512 devices in a mesh: cols: 16 (over y_lo, x, core), trc: 16 (over z), lev: 2 (over y_hi).
Axes of the slice: x: 4, y: 4 (y_hi: 2, y_lo: 2; y = y_hi * 2 + y_lo), z: 16, core: 2. Of those that a mesh axis runs over, the one named last changes fastest.
Arguments:
- potential_warmth: float32 [128, 128, 128], P('lev', 'cols', 'trc'), may hold values from -6 to 6
- saltiness_anomaly: float32 [128, 128, 128], P('lev', 'cols', 'trc'), may hold values from -6 to 6
- zonal_speed: float32 [128, 128, 128], P('lev', 'cols', 'trc'), may hold values from -3 to 3
- meridional_speed: float32 [128, 128, 128], P('lev', 'cols', 'trc'), may hold values from -3 to 3
- marine_indicator: int32 [128, 128, 128], P('lev', 'cols', 'trc'), may hold values from 0 to 1, as said below
- species_concentrations: float32 [64, 128, 128, 128], P('trc', 'lev', 'cols'), may hold values from 0.1 to 2
- coupling_matrix: bfloat16 [64, 64], replicated, may hold values from -0.75 to 0.75
- species_guild_number: int32 [64], replicated, may hold values from 0 to 7
- guild_extinction_coefficient: float32 [8], replicated, may hold values from 0.0001 to 0.0012
Outputs:
- warmth_final: float32 [128, 128, 128], P('lev', 'cols', 'trc')
- saltiness_final: float32 [128, 128, 128], P('lev', 'cols', 'trc')
- zonal_speed_final: float32 [128, 128, 128], P('lev', 'cols', 'trc')
- meridional_speed_final: float32 [128, 128, 128], P('lev', 'cols', 'trc')
- species_final: float32 [64, 128, 128, 128], P('trc', 'lev', 'cols')
The draws below stay inside these ranges and needn't reach their ends.
Inputs may be any that keep to these rules, and one draw needn't show every extreme that they name: `marine_indicator`: each column is sea from level 0 down to a depth drawn per column and land below it; the columns at the first index and at the last two indices of the second horizontal dimension are sea at every level.
All inputs are finite; a program needn't handle non-finite values.
Results may differ from the reference program's by a relative error of at most 0.00066.
Values may be sent and summed in bfloat16 or wider, within the bound.
A program may use at most 64 MiB of HBM per device.

```python
import math
import jax
import jax.numpy as jnp
from jax import lax

NT = 64
NGRP = 8
ZONAL_POINTS = 128
MERIDIONAL_POINTS = 128
DEPTH_LAYERS = 128


def draw_marine_indicator(key, part):
    column_depth = jax.random.randint(key, (ZONAL_POINTS, MERIDIONAL_POINTS), -(DEPTH_LAYERS // 4), DEPTH_LAYERS + 1)
    column_depth = jnp.maximum(column_depth, 0)
    row_index = lax.broadcasted_iota(jnp.int32, (ZONAL_POINTS, MERIDIONAL_POINTS), 1)
    full_sea = (row_index == 0) | (row_index >= MERIDIONAL_POINTS - 2)
    column_depth = jnp.where(full_sea, DEPTH_LAYERS, column_depth)
    level_index = lax.broadcasted_iota(jnp.int32, (DEPTH_LAYERS, ZONAL_POINTS, MERIDIONAL_POINTS), 0)
    return (level_index < column_depth[None]).astype(jnp.int32)


def with_ends(entries, own_key, smallest, largest):
    longest = entries.shape.index(max(entries.shape))
    spots = []
    for shift in (0, 1):
        where = [jax.random.randint(jax.random.fold_in(own_key, axis), (), 0, length) for axis, length in enumerate(entries.shape)]
        where[longest] = (where[longest] + shift) % entries.shape[longest]
        spots.append(tuple(where))
    return entries.at[spots[0]].set(smallest).at[spots[1]].set(largest)


def steps_of(rng, shape, shards, smallest, high):
    loudness, own = 1.0, jax.random.fold_in(rng, 6)
    for axis_at, parts in shards:
        draws = jnp.exp(jax.random.uniform(jax.random.fold_in(own, axis_at), (parts,), jnp.float32, smallest / len(shards), high / len(shards)))
        loudness = loudness * jnp.repeat(draws, shape[axis_at] // parts).reshape([-1 if axis == axis_at else 1 for axis in range(len(shape))])
    return loudness


def scatter_about(rng, shape, spread, bound, shards=(), dtype=jnp.bfloat16):
    values = jax.random.normal(rng, shape, jnp.float32) * spread
    if len(shards) > 0:
        values = steps_of(rng, shape, shards, -0.22, 0.18) * values
    return jnp.clip(values, min=-bound, max=bound).astype(dtype)


def setup_inputs(seed: int = 0) -> dict:
    arg_keys = jax.random.split(jax.random.key(seed), 10)
    potential_warmth = scatter_about(arg_keys[0], (DEPTH_LAYERS, ZONAL_POINTS, MERIDIONAL_POINTS), 1.0, 6.0, ((0, 2), (1, 16), (2, 16)), jnp.float32)
    saltiness_anomaly = scatter_about(arg_keys[1], (DEPTH_LAYERS, ZONAL_POINTS, MERIDIONAL_POINTS), 1.0, 6.0, ((0, 2), (1, 16), (2, 16)), jnp.float32)
    zonal_speed = scatter_about(arg_keys[2], (DEPTH_LAYERS, ZONAL_POINTS, MERIDIONAL_POINTS), 0.5, 3.0, ((0, 2), (1, 16), (2, 16)), jnp.float32)
    meridional_speed = scatter_about(arg_keys[3], (DEPTH_LAYERS, ZONAL_POINTS, MERIDIONAL_POINTS), 0.5, 3.0, ((0, 2), (1, 16), (2, 16)), jnp.float32)
    marine_indicator = draw_marine_indicator(jax.random.fold_in(arg_keys[9], 71), 0)
    species_concentrations = jnp.clip(jnp.exp(math.log(2.0) - 2.9957323 * jax.random.uniform(arg_keys[5], (NT, DEPTH_LAYERS, ZONAL_POINTS, MERIDIONAL_POINTS), jnp.float32) ** steps_of(arg_keys[5], (NT, DEPTH_LAYERS, ZONAL_POINTS, MERIDIONAL_POINTS), ((0, 16), (1, 2), (2, 16)), -0.2, 0.2)), 0.1, 2.0)
    coupling_matrix = scatter_about(arg_keys[6], (NT, NT), NT ** -0.5, 0.75)
    species_guild_number = with_ends(jax.random.randint(arg_keys[7], (NT,), 0, NGRP), jax.random.fold_in(arg_keys[7], 1), 0, NGRP - 1).astype(jnp.int32)
    guild_extinction_coefficient = jnp.clip(jnp.exp(jax.random.uniform(arg_keys[8], (NGRP,), jnp.float32, math.log(0.0001), math.log(0.0012))), 0.0001, 0.0012)
    return dict(potential_warmth=potential_warmth, saltiness_anomaly=saltiness_anomaly, zonal_speed=zonal_speed, meridional_speed=meridional_speed, marine_indicator=marine_indicator, species_concentrations=species_concentrations, coupling_matrix=coupling_matrix, species_guild_number=species_guild_number, guild_extinction_coefficient=guild_extinction_coefficient)


viscosity = 0.2
buoyancy = 0.25
marine_advance = 0.05
tracer_step = 0.2
level_step = 0.04
react_step = 0.25
warming_amount = 60.0


def minmod(slope_left, slope_right):
    return 0.5 * (jnp.sign(slope_left) + jnp.sign(slope_right)) * jnp.minimum(jnp.abs(slope_left), jnp.abs(slope_right))


def limited_div(padded, face_speed, dimension):
    length = padded.shape[dimension] - 4
    far_left = lax.slice_in_dim(padded, 0, length + 1, axis=dimension)
    left_cell = lax.slice_in_dim(padded, 1, length + 2, axis=dimension)
    right_cell = lax.slice_in_dim(padded, 2, length + 3, axis=dimension)
    far_right = lax.slice_in_dim(padded, 3, length + 4, axis=dimension)
    plus_side = left_cell + 0.5 * minmod(left_cell - far_left, right_cell - left_cell)
    minus_side = right_cell - 0.5 * minmod(right_cell - left_cell, far_right - right_cell)
    face_flux = jnp.maximum(face_speed, 0.0) * plus_side + jnp.minimum(face_speed, 0.0) * minus_side
    return lax.slice_in_dim(face_flux, 1, length + 1, axis=dimension) - lax.slice_in_dim(face_flux, 0, length, axis=dimension)


def shift_east(values):
    return jnp.roll(values, -1, 1)


def shift_west(values):
    return jnp.roll(values, 1, 1)


def shift_north(values):
    return jnp.roll(values, -1, 2)


def shift_south(values):
    return jnp.roll(values, 1, 2)


def reference(potential_warmth, saltiness_anomaly, zonal_speed, meridional_speed, marine_indicator, species_concentrations, coupling_matrix, species_guild_number, guild_extinction_coefficient):
    marine_indicator_real = marine_indicator.astype(jnp.float32)
    fluid_mass_per_volume = 0.8 * saltiness_anomaly - 0.2 * potential_warmth
    hydrostatic_pressure = buoyancy * (jnp.cumsum(fluid_mass_per_volume, axis=0) - 0.5 * fluid_mass_per_volume)
    mask_east = marine_indicator_real * shift_east(marine_indicator_real)
    mask_north = marine_indicator_real * shift_north(marine_indicator_real)
    east_laplace = shift_east(zonal_speed) + shift_west(zonal_speed) + shift_north(zonal_speed) + shift_south(zonal_speed) - 4.0 * zonal_speed
    north_laplace = shift_east(meridional_speed) + shift_west(meridional_speed) + shift_north(meridional_speed) + shift_south(meridional_speed) - 4.0 * meridional_speed
    zonal_speed_final = mask_east * (zonal_speed + marine_advance * (-(shift_east(hydrostatic_pressure) - hydrostatic_pressure) + viscosity * east_laplace))
    meridional_speed_final = mask_north * (meridional_speed + marine_advance * (-(shift_north(hydrostatic_pressure) - hydrostatic_pressure) + viscosity * north_laplace))
    divergence = zonal_speed_final - shift_west(zonal_speed_final) + meridional_speed_final - shift_south(meridional_speed_final)
    deeper_sum = jnp.cumsum(divergence[::-1], axis=0)[::-1]
    level_index = lax.broadcasted_iota(jnp.int32, divergence.shape, 0)
    faces_vertical = jnp.concatenate([jnp.where(level_index == 0, 0.0, deeper_sum), jnp.zeros_like(deeper_sum[:1])], axis=0)

    def donor_quantity(values):
        flux_east = jnp.maximum(zonal_speed_final, 0.0) * values + jnp.minimum(zonal_speed_final, 0.0) * shift_east(values)
        flux_north = jnp.maximum(meridional_speed_final, 0.0) * values + jnp.minimum(meridional_speed_final, 0.0) * shift_north(values)
        padded = jnp.pad(values, ((1, 1), (0, 0), (0, 0)))
        flux_down = jnp.maximum(faces_vertical, 0.0) * padded[:-1] + jnp.minimum(faces_vertical, 0.0) * padded[1:]
        return (flux_east - shift_west(flux_east)) + (flux_north - shift_south(flux_north)) + (flux_down[1:] - flux_down[:-1])

    faces_east = jnp.concatenate([zonal_speed_final[:, -1:], zonal_speed_final], axis=1)
    faces_north = jnp.concatenate([meridional_speed_final[:, :, -1:], meridional_speed_final], axis=2)

    def advect(values):
        for repeat in range(2):
            beside = jnp.concatenate([values[:, -2:], values, values[:, :2]], axis=1)
            beside_all = jnp.concatenate([values[:, :, -2:], values, values[:, :, :2]], axis=2)
            stacks = jnp.pad(values, ((2, 2), (0, 0), (0, 0)))
            sideways = limited_div(beside, faces_east, 1) + limited_div(beside_all, faces_north, 2)
            upright = limited_div(stacks, faces_vertical, 0)
            values = values - (tracer_step * sideways + level_step * upright)
        return values

    advected = lax.map(advect, species_concentrations)
    onehot = (species_guild_number[:, None] == lax.broadcasted_iota(jnp.int32, (species_guild_number.shape[0], guild_extinction_coefficient.shape[0]), 1)).astype(jnp.float32)
    absorb = jnp.sum(onehot * guild_extinction_coefficient[None, :], axis=1)

    def per_level(level_block):
        rounded = lax.optimization_barrier(level_block.astype(jnp.bfloat16))
        flattened = rounded.reshape(rounded.shape[0], -1)
        reaction = jnp.dot(coupling_matrix, flattened, preferred_element_type=jnp.float32).reshape(level_block.shape)
        updated = level_block + react_step * reaction
        attenuation = jnp.sum(absorb[:, None, None] * rounded.astype(jnp.float32), axis=0)
        return updated, attenuation

    updated, attenuation = lax.map(per_level, jnp.swapaxes(advected, 0, 1))
    species_final = jnp.swapaxes(updated, 0, 1)
    light_path = jnp.cumsum(attenuation, axis=0) - attenuation
    radiation_captured = jnp.exp(-light_path) * (1.0 - jnp.exp(-attenuation))
    warmth_final = potential_warmth - marine_advance * donor_quantity(potential_warmth) + warming_amount * marine_indicator_real * radiation_captured
    saltiness_final = saltiness_anomaly - marine_advance * donor_quantity(saltiness_anomaly)
    return warmth_final, saltiness_final, zonal_speed_final, meridional_speed_final, species_final
```

```python
import functools

import jax
import jax.numpy as jnp
from jax import lax
from jax.experimental import pallas as pl
from jax.experimental.pallas import tpu as pltpu
from jax.sharding import PartitionSpec as P

MESH = pl.DeviceIdType.MESH
F32 = jnp.float32
BF16 = jnp.bfloat16
VMEM = pl.BlockSpec(memory_space=pltpu.VMEM)

viscosity = 0.2
buoyancy = 0.25
marine_advance = 0.05
tracer_step = 0.2
level_step = 0.04
react_step = 0.25
warming_amount = 60.0

LOW, AUX, HIGH = 0, 1024, 1152
BLOCK = 2176
PART = 1152


def sds(shape, dtype=F32):
    return jax.ShapeDtypeStruct(shape, dtype)


def iota(shape, axis):
    return lax.broadcasted_iota(jnp.int32, shape, axis)


def pieces(value):
    first = value.astype(BF16)
    rest = value - first.astype(F32)
    second = rest.astype(BF16)
    third = (rest - second.astype(F32)).astype(BF16)
    return first, second, third


def minmod_half(left, right):
    return jnp.maximum(jnp.minimum(left, right), jnp.minimum(jnp.maximum(left, right), 0.0))


def pack_kernel(t_ref, s_ref, u_ref, v_ref, m_ref, above_ref, sp_ref, b_ref, xs_ref):
    for f, ref in enumerate((t_ref, s_ref, u_ref, v_ref)):
        for k in range(4):
            off = (LOW if k < 2 else HIGH) + f * 256 + (k % 2) * 128
            b_ref[:, off : off + 128] = jnp.concatenate([ref[2 * k], ref[2 * k + 1]], axis=1)
    lane = iota((8, 128), 1)
    aux = above_ref[...]
    for x in range(8):
        count = jnp.sum(m_ref[x].astype(F32), axis=1, keepdims=True)
        aux = aux + jnp.where(lane == x, count, 0.0)
    b_ref[:, AUX : AUX + 128] = aux

    def one(t, carry):
        for x in range(8):
            xs_ref[t, x] = sp_ref[t, pl.ds(x, 64, stride=8), :]
        return carry

    lax.fori_loop(0, 4, one, 0)


def gather_kernel(nz, nx, b_ref, xs_ref, g_ref, gl_ref, gh_ref, se_ref, zs, zr, ls, lr, hs, hr, ss, sr):
    z, x, lev = lax.axis_index("trc"), lax.axis_index("cols"), lax.axis_index("lev")
    zup, zdn = {"trc": (z + 1) % nz}, {"trc": (z + nz - 1) % nz}
    xup, xdn = {"cols": (x + 1) % nx}, {"cols": (x + nx - 1) % nx}
    peer = {"lev": 1 - lev}
    barrier = pltpu.get_barrier_semaphore()
    for other in (zup, zdn, xup, xdn, peer):
        pl.semaphore_signal(barrier, inc=1, device_id=other, device_id_type=MESH)
    pl.semaphore_wait(barrier, 5)

    def rdma(src, dst, send, recv, to):
        return pltpu.make_async_remote_copy(
            src_ref=src, dst_ref=dst, send_sem=send, recv_sem=recv, device_id=to, device_id_type=MESH
        )

    def along(src, source, way):
        return rdma(src, g_ref.at[source], zs.at[way, source], zr.at[source], zup if way == 0 else zdn)

    def to_right(src, source):
        return rdma(src.at[:, AUX:], gl_ref.at[source], ls.at[source], lr.at[source], xup)

    def to_left(src, source):
        return rdma(src.at[:, :PART], gh_ref.at[source], hs.at[source], hr.at[source], xdn)

    along(b_ref, z, 0).start()
    along(b_ref, z, 1).start()
    to_right(b_ref, z).start()
    to_left(b_ref, z).start()

    near = pl.multiple_of((1 - lev) * 56, 8)
    there = pl.multiple_of((1 - lev) * 0 + lev * 72, 8)
    nothing = pl.multiple_of(lev * 72, 8)
    own_x = rdma(xs_ref.at[:, 4:8], se_ref.at[:, 0:4, 8:72], ss.at[0], sr.at[0], xup)
    own_y = rdma(xs_ref.at[:, 0:4], se_ref.at[:, 12:16, 8:72], ss.at[1], sr.at[1], xdn)
    own_l = rdma(xs_ref.at[:, :, pl.ds(near, 8)], se_ref.at[:, 4:12, pl.ds(there, 8)], ss.at[2], sr.at[2], peer)
    own_x.start()
    own_y.start()
    own_l.start()

    g_ref[z] = b_ref[...]

    def keep(t, carry):
        se_ref[t, 4:12, 8:72, :] = xs_ref[t]
        se_ref[t, :, pl.ds(nothing, 8), :] = jnp.zeros((16, 8, 128), F32)
        return carry

    lax.fori_loop(0, 4, keep, 0)

    near_e = pl.multiple_of(near + 8, 8)
    low_l = rdma(se_ref.at[:, 0:4, pl.ds(near_e, 8)], se_ref.at[:, 0:4, pl.ds(there, 8)], ss.at[3], sr.at[3], peer)
    high_l = rdma(se_ref.at[:, 12:16, pl.ds(near_e, 8)], se_ref.at[:, 12:16, pl.ds(there, 8)], ss.at[4], sr.at[4], peer)

    half = nz // 2
    for step in range(1, half + 1):
        source = (z + nz - step) % nz
        block = g_ref.at[source]
        along(block, source, 0).wait_recv()
        if step < half:
            along(block, source, 0).start()
        to_right(block, source).start()
        to_left(block, source).start()
        if step < half:
            source = (z + step) % nz
            block = g_ref.at[source]
            along(block, source, 1).wait_recv()
            if step < half - 1:
                along(block, source, 1).start()
            to_right(block, source).start()
            to_left(block, source).start()
        if step == half // 2:
            own_x.wait_recv()
            low_l.start()
            own_y.wait_recv()
            high_l.start()

    own_l.wait_recv()
    low_l.wait_recv()
    high_l.wait_recv()

    def arrived(source, carry):
        to_right(b_ref, source).wait_recv()
        to_left(b_ref, source).wait_recv()
        to_right(b_ref, source).wait_send()
        to_left(b_ref, source).wait_send()
        return carry

    lax.fori_loop(0, nz, arrived, 0)
    for step in range(half):
        along(b_ref, (z + nz - step) % nz, 0).wait_send()
    for step in range(half - 1):
        along(b_ref, (z + step) % nz, 1).wait_send()
    for copy in (own_x, own_y, own_l, low_l, high_l):
        copy.wait_send()


def flow_kernel(g_ref, gl_ref, gh_ref, uf_ref, vf_ref, fv_ref, t_ref, s_ref, bnd_ref, rho, uu, vv, pp, cnt, top):
    lev = lax.axis_index("lev")
    fields = (t_ref, s_ref, uu, vv)
    sides = ((gl_ref, 128), (g_ref, LOW), (g_ref, HIGH), (gh_ref, 0))
    for part, (ref, base) in enumerate(sides):
        for f, out in enumerate(fields):
            for k in range(2):
                off = base + f * 256 + k * 128
                r = part * 4 + k * 2
                out[r : r + 2] = ref[:, off : off + 128].T.reshape(2, 64, 128)
    aux, aux_l, aux_h = g_ref[:, AUX:HIGH].T, gl_ref[:, 0:128].T, gh_ref[:, AUX:HIGH].T
    cnt[0:4], cnt[4:12], cnt[12:16] = aux_l[4:8], aux[0:8], aux_h[0:4]
    top[0:4], top[4:12], top[12:16] = aux_l[12:16], aux[8:16], aux_h[8:12]

    row, col = iota((64, 64), 0), iota((64, 64), 1)
    down = jnp.where(col < row, 1.0, jnp.where(col == row, 0.5, 0.0)).astype(BF16)
    down = jnp.concatenate([down] * 3, axis=1)
    deep = jnp.where(col >= row, 1.0, 0.0).astype(BF16)
    deep = jnp.concatenate([deep] * 3, axis=1)
    for r in range(16):
        dense = 0.8 * s_ref[r] - 0.2 * t_ref[r]
        total = jnp.dot(down, jnp.concatenate(pieces(dense), axis=0), preferred_element_type=F32)
        pp[r] = buoyancy * (top[r : r + 1] + total)

    level = iota((64, 128), 0).astype(F32)
    uf_ref[0] = jnp.zeros((64, 128), F32)
    vf_ref[0] = jnp.zeros((64, 128), F32)
    for r in (14, 15):
        uf_ref[r] = jnp.zeros((64, 128), F32)
        vf_ref[r] = jnp.zeros((64, 128), F32)
    for r in range(1, 14):
        here, east = cnt[r : r + 1], cnt[r + 1 : r + 2]
        north = pltpu.roll(jnp.broadcast_to(here, (8, 128)), 127, 1)[0:1]
        p, u, v = pp[r], uu[r], vv[r]
        lap_u = uu[r + 1] + uu[r - 1] + pltpu.roll(u, 127, 1) + pltpu.roll(u, 1, 1) - 4.0 * u
        lap_v = vv[r + 1] + vv[r - 1] + pltpu.roll(v, 127, 1) + pltpu.roll(v, 1, 1) - 4.0 * v
        new_u = u + marine_advance * (p - pp[r + 1] + viscosity * lap_u)
        new_v = v + marine_advance * (p - pltpu.roll(p, 127, 1) + viscosity * lap_v)
        uf_ref[r] = jnp.where(level < jnp.minimum(here, east), new_u, 0.0)
        vf_ref[r] = jnp.where(level < jnp.minimum(here, north), new_v, 0.0)

    zero = jnp.zeros((1, 128), F32)
    first = lev == 0
    for r in range(16):
        if 2 <= r < 14:
            u, v = uf_ref[r], vf_ref[r]
            div = u - uf_ref[r - 1] + v - pltpu.roll(v, 1, 1)
            fv = jnp.dot(deep, jnp.concatenate(pieces(div), axis=0), preferred_element_type=F32)
            fv_ref[r] = fv
            flow = fv[0:1]
        else:
            fv_ref[r] = jnp.zeros((64, 128), F32)
            flow = zero
        u2 = jnp.where(first, uf_ref[r, 62:64], uf_ref[r, 0:2])
        v2 = jnp.where(first, vf_ref[r, 62:64], vf_ref[r, 0:2])
        t1 = jnp.where(first, t_ref[r, 63:64], t_ref[r, 0:1])
        s1 = jnp.where(first, s_ref[r, 63:64], s_ref[r, 0:1])
        bnd_ref[r] = jnp.concatenate([u2, v2, flow, t1, s1, zero], axis=0)


def advect_kernel(
    uf_ref, vf_ref, fv_ref, t_ref, s_ref, bnd_ref, se_ref, adv_ref, send_ref, oc_ref, up, um, vp, vm, fp, fm, q1, ex, tr
):
    z, lev = lax.axis_index("trc"), lax.axis_index("lev")
    first = lev == 0
    sub = iota((8, 128), 0)

    def around(own, above, below):
        return jnp.concatenate(
            [jnp.where(first, 0.0, above), own, jnp.where(first, below, 0.0)], axis=0
        )

    def faces(r, carry):
        edge = bnd_ref[r]
        edge_w = bnd_ref[r - 1]
        pos = pltpu.roll(edge, 6, 0)
        u_ext = around(uf_ref[r], jnp.where(sub >= 6, pos, 0.0), jnp.where(sub < 2, edge, 0.0))
        two = pltpu.roll(edge, 4, 0)
        low = pltpu.roll(edge, 6, 0)
        v_ext = around(vf_ref[r], jnp.where(sub >= 6, two, 0.0), jnp.where(sub < 2, low, 0.0))
        d2 = edge[0:2] - edge_w[0:2] + edge[2:4] - pltpu.roll(edge, 1, 1)[2:4]
        d0, d1 = d2[0:1], d2[1:2]
        flow = jnp.where(first, edge[4:5], 0.0)
        f_own = fv_ref[r] + flow
        above = jnp.where(sub == 7, f_own[0:1] + d1, jnp.where(sub == 6, f_own[0:1] + d1 + d0, 0.0))
        below = jnp.where(
            sub == 0, flow, jnp.where(sub == 1, flow - d0, jnp.where(sub == 2, flow - d0 - d1, 0.0))
        )
        surface = jnp.where((iota((64, 128), 0) == 0) & first, 0.0, f_own)
        f_ext = level_step * around(surface, above, below)
        u_ext = tracer_step * u_ext
        v_ext = tracer_step * v_ext
        up[r], um[r] = jnp.maximum(u_ext, 0.0), jnp.minimum(u_ext, 0.0)
        vp[r], vm[r] = jnp.maximum(v_ext, 0.0), jnp.minimum(v_ext, 0.0)
        fp[r], fm[r] = jnp.maximum(f_ext, 0.0), jnp.minimum(f_ext, 0.0)
        return carry

    lax.fori_loop(1, 14, faces, 0)

    def sweep(load, store, start, stop):
        d_a = 0.5 * (load(start - 1) - load(start - 2))
        d_b = 0.5 * (load(start) - load(start - 1))
        d_c = 0.5 * (load(start + 1) - load(start))
        right = load(start - 1) + minmod_half(d_a, d_b)
        slope = minmod_half(d_b, d_c)
        flux = up[start - 1] * right + um[start - 1] * (load(start) - slope)

        def one(r, carry):
            d_here, right, flux = carry
            q, q_e = load(r), load(r + 1)
            d_next = 0.5 * (load(r + 2) - q_e)
            slope = minmod_half(d_here, d_next)
            flux_e = up[r] * right + um[r] * (q_e - slope)
            change = flux_e - flux
            right_e = q_e + slope
            north = 0.5 * (pltpu.roll(q, 127, 1) - q)
            slope = minmod_half(pltpu.roll(north, 1, 1), north)
            flux_n = vp[r] * (q + slope) + vm[r] * pltpu.roll(q - slope, 127, 1)
            change = change + (flux_n - pltpu.roll(flux_n, 1, 1))
            below = 0.5 * (pltpu.roll(q, 79, 0) - q)
            slope = minmod_half(pltpu.roll(below, 1, 0), below)
            flux_v = fp[r] * pltpu.roll(q + slope, 1, 0) + fm[r] * (q - slope)
            change = change + (pltpu.roll(flux_v, 79, 0) - flux_v)
            store(r, q - change)
            return d_next, right_e, flux_e

        lax.fori_loop(start, stop, one, (d_c, load(start) + slope, flux))

    def tracer(t, carry):
        def first_load(r):
            return se_ref[t, r]

        def first_store(r, value):
            q1[r] = value

        def second_load(r):
            return q1[r]

        def second_store(r, value):
            adv_ref[t, r - 4] = value[8:72]

        sweep(first_load, first_store, 2, 14)
        sweep(second_load, second_store, 4, 12)
        return carry

    lax.fori_loop(0, 4, tracer, 0)

    def pair(tp, carry):
        for k in range(4):
            one = adv_ref[2 * tp, 2 * k : 2 * k + 2].reshape(128, 128).T.reshape(16, 8, 128)
            two = adv_ref[2 * tp + 1, 2 * k : 2 * k + 2].reshape(128, 128).T.reshape(16, 8, 128)
            send_ref[k, :, tp] = jnp.concatenate([one, two], axis=1).astype(BF16)
        return carry

    lax.fori_loop(0, 2, pair, 0)

    mine = pl.multiple_of(z * 8, 8)
    for f, ref in enumerate((t_ref, s_ref)):
        for r in range(3, 13):
            edge = bnd_ref[r][5 + f : 6 + f]
            ex[r] = around(ref[r], jnp.where(sub == 7, edge, 0.0), jnp.where(sub == 0, edge, 0.0))

        def donor(r, flux_w):
            c = ex[r]
            flux = up[r] * c + um[r] * ex[r + 1]
            flux_n = vp[r] * c + vm[r] * pltpu.roll(c, 127, 1)
            flux_v = fp[r] * pltpu.roll(c, 1, 0) + fm[r] * c
            wide = flux - flux_w + (flux_n - pltpu.roll(flux_n, 1, 1))
            tall = pltpu.roll(flux_v, 79, 0) - flux_v
            new = c - (marine_advance / tracer_step) * wide - (marine_advance / level_step) * tall
            q1[r] = new
            return flux

        lax.fori_loop(4, 12, donor, up[3] * ex[3] + um[3] * ex[4])
        for k in range(4):
            both = jnp.concatenate([q1[4 + 2 * k, 8:72], q1[5 + 2 * k, 8:72]], axis=0)
            tr[...] = both.T
            oc_ref[f, :, k * 128 : k * 128 + 128] = tr[pl.ds(mine, 8), :]
    for f, ref in enumerate((uf_ref, vf_ref)):
        for k in range(4):
            tr[...] = ref[4 + 2 * k : 6 + 2 * k].reshape(128, 128).T
            oc_ref[2 + f, :, k * 128 : k * 128 + 128] = tr[pl.ds(mine, 8), :]


def matrix_kernel(c_ref, absorb_ref, w_ref):
    spread = jnp.where(iota((512, 64), 0) // 8 == iota((512, 64), 1), 1.0, 0.0).astype(BF16)
    across = jnp.where(iota((64, 512), 1) // 8 == iota((64, 512), 0), 1.0, 0.0).astype(BF16)
    tall = jnp.dot(spread, c_ref[...], preferred_element_type=F32).astype(BF16)
    wide = jnp.dot(tall, across, preferred_element_type=F32)
    w_ref[0:512] = jnp.where(iota((512, 512), 0) % 8 == iota((512, 512), 1) % 8, wide, 0.0).astype(BF16)
    own = iota((8, 512), 0) == iota((8, 512), 1) % 8
    rows = []
    for part in pieces(absorb_ref[...]):
        line = jnp.dot(part, across, preferred_element_type=F32)
        rows.append(jnp.where(own, line, 0.0))
    rows.append(jnp.zeros((8, 512), F32))
    w_ref[512:544] = jnp.concatenate(rows, axis=0).astype(BF16)


def react_kernel(nz, send_ref, w_ref, back_ref, att_ref, attp_ref, got, res, s1, r1, s2, r2, s3, r3):
    z, lev = lax.axis_index("trc"), lax.axis_index("lev")
    peer = {"lev": 1 - lev}
    barrier = pltpu.get_barrier_semaphore()

    def greet(d, carry):
        pl.semaphore_signal(barrier, inc=1, device_id={"trc": (z + d) % nz}, device_id_type=MESH)
        return carry

    lax.fori_loop(1, nz, greet, 0)
    pl.semaphore_signal(barrier, inc=1, device_id=peer, device_id_type=MESH)
    pl.semaphore_wait(barrier, nz)

    def rdma(src, dst, send, recv, to):
        return pltpu.make_async_remote_copy(
            src_ref=src, dst_ref=dst, send_sem=send, recv_sem=recv, device_id=to, device_id_type=MESH
        )

    def out(c, d):
        to = (z + d) % nz
        return rdma(send_ref.at[c, to], got.at[c, z], s1.at[c, d], r1.at[c, z], {"trc": to})

    def came(c, d):
        source = (z + d) % nz
        return rdma(send_ref.at[c, source], got.at[c, source], s1.at[c, d], r1.at[c, source], {"trc": source})

    def home(c, d):
        to = (z + d) % nz
        return rdma(res.at[c, to], back_ref.at[c, z], s2.at[c, d], r2.at[c, z], {"trc": to})

    def homed(c, d):
        source = (z + d) % nz
        return rdma(res.at[c, source], back_ref.at[c, source], s2.at[c, d], r2.at[c, source], {"trc": source})

    for c in range(4):
        lax.fori_loop(1, nz, lambda d, carry: (out(c, d).start(), carry)[1], 0)
        got[c, z] = send_ref[c, z]
    for c in range(4):
        lax.fori_loop(1, nz, lambda d, carry: (came(c, d).wait_recv(), carry)[1], 0)
        values = jnp.dot(w_ref[...], got[c].reshape(512, 128), preferred_element_type=F32)
        res[c] = values[0:512].reshape(nz, 32, 128)
        att_ref[c] = values[512:520] + values[520:528] + values[528:536]
        lax.fori_loop(1, nz, lambda d, carry: (home(c, d).start(), carry)[1], 0)
        back_ref[c, z] = res[c, z]
    shade = rdma(att_ref, attp_ref, s3, r3, peer)
    shade.start()
    for c in range(4):

        def finish(d, carry):
            homed(c, d).wait_recv()
            out(c, d).wait_send()
            home(c, d).wait_send()
            return carry

        lax.fori_loop(1, nz, finish, 0)
    shade.wait_recv()
    shade.wait_send()


def final_kernel(adv_ref, back_ref, att_ref, attp_ref, oc_ref, m_ref, w_ref, s_ref, u_ref, v_ref, sp_ref):
    lev = lax.axis_index("lev")

    def one(t, carry):
        at = pl.multiple_of(t * 8, 8)
        for c in range(4):
            react = back_ref[c, :, pl.ds(at, 8), :].reshape(128, 128).T
            new = adv_ref[t, 2 * c : 2 * c + 2].reshape(128, 128) + react_step * react
            sp_ref[t, pl.ds(2 * c, 64, stride=8), :] = new[0:64]
            sp_ref[t, pl.ds(2 * c + 1, 64, stride=8), :] = new[64:128]
        return carry

    lax.fori_loop(0, 4, one, 0)
    row, col = iota((128, 128), 0), iota((128, 128), 1)
    same = row // 64 == col // 64
    before = jnp.where(same & (row < col), 1.0, 0.0).astype(BF16)
    every = jnp.where(same & (lev == 1), 1.0, 0.0).astype(BF16)
    sums = jnp.concatenate([before] * 3 + [every] * 3, axis=0)
    for c in range(4):
        att = att_ref[c]
        terms = jnp.concatenate(pieces(att) + pieces(attp_ref[c]), axis=1)
        path = jnp.dot(terms, sums, preferred_element_type=F32)
        caught = jnp.exp(-path) * (1.0 - jnp.exp(-att))
        wet = jnp.concatenate([m_ref[2 * c], m_ref[2 * c + 1]], axis=1).astype(F32)
        lanes = slice(c * 128, c * 128 + 128)
        warm = oc_ref[0, :, lanes] + warming_amount * wet * caught
        for out, value in ((w_ref, warm), (s_ref, oc_ref[1, :, lanes]), (u_ref, oc_ref[2, :, lanes]), (v_ref, oc_ref[3, :, lanes])):
            out[2 * c] = value[:, 0:64]
            out[2 * c + 1] = value[:, 64:128]


def plain(kernel, outs, scratch=(), name=None):
    return pl.pallas_call(
        kernel,
        out_shape=outs,
        out_specs=jax.tree.map(lambda _: VMEM, outs),
        scratch_shapes=list(scratch),
        compiler_params=pltpu.CompilerParams(vmem_limit_bytes=48 << 20),
        name=name,
    )


def shards(
    nz,
    nx,
    potential_warmth,
    saltiness_anomaly,
    zonal_speed,
    meridional_speed,
    marine_indicator,
    species_concentrations,
    coupling_matrix,
    species_guild_number,
    guild_extinction_coefficient,
):
    tiles = [
        jnp.transpose(a, (1, 2, 0))
        for a in (potential_warmth, saltiness_anomaly, zonal_speed, meridional_speed, marine_indicator)
    ]
    dense = jnp.sum(0.8 * tiles[1] - 0.2 * tiles[0], axis=2)
    above = lax.ppermute(dense, "lev", [(0, 1)])
    above = jnp.pad(above.T, ((0, 0), (8, 112)))
    species = species_concentrations.reshape(4, 512, 128)
    block, xs = plain(pack_kernel, (sds((8, BLOCK)), sds((4, 8, 64, 128))), name="pack")(*tiles, above, species)

    dma = pltpu.SemaphoreType.DMA
    gathered, left, right, ext = pl.pallas_call(
        functools.partial(gather_kernel, nz, nx),
        out_shape=(sds((nz, 8, BLOCK)), sds((nz, 8, PART)), sds((nz, 8, PART)), sds((4, 16, 80, 128))),
        in_specs=[VMEM] * 2,
        out_specs=(VMEM,) * 4,
        scratch_shapes=[dma((2, nz)), dma((nz,)), dma((nz,)), dma((nz,)), dma((nz,)), dma((nz,)), dma((5,)), dma((5,))],
        compiler_params=pltpu.CompilerParams(collective_id=0, has_side_effects=True, vmem_limit_bytes=48 << 20),
        name="gather",
    )(block, xs)

    row = sds((16, 64, 128))
    big = pltpu.VMEM((16, 64, 128), F32)
    small = pltpu.VMEM((16, 128), F32)
    uf, vf, fv, t_ext, s_ext, edge = plain(
        flow_kernel, (row, row, row, row, row, sds((16, 8, 128))), [big, big, big, big, small, small], name="flow"
    )(gathered.reshape(128, BLOCK), left.reshape(128, PART), right.reshape(128, PART))
    edge = lax.ppermute(edge, "lev", [(0, 1), (1, 0)])

    tall = pltpu.VMEM((16, 80, 128), F32)
    adv, send, ocean = plain(
        advect_kernel,
        (sds((4, 8, 64, 128)), sds((4, nz, 2, 16, 128), BF16), sds((4, 8, 512))),
        [tall] * 8 + [pltpu.VMEM((128, 128), F32)],
        name="advect",
    )(uf, vf, fv, t_ext, s_ext, edge, ext)

    onehot = species_guild_number[None, :] == lax.broadcasted_iota(jnp.int32, (8, 64), 0)
    absorb = jnp.sum(jnp.where(onehot, guild_extinction_coefficient[:, None], 0.0), axis=0, keepdims=True)
    absorb = jnp.broadcast_to(absorb, (8, 64))
    matrix = plain(matrix_kernel, sds((544, 512), BF16), name="matrix")(coupling_matrix, absorb)

    back, att, attp = pl.pallas_call(
        functools.partial(react_kernel, nz),
        out_shape=(sds((4, nz, 32, 128)), sds((4, 8, 128)), sds((4, 8, 128))),
        in_specs=[VMEM] * 2,
        out_specs=(VMEM,) * 3,
        scratch_shapes=[
            pltpu.VMEM((4, nz, 2, 16, 128), BF16),
            pltpu.VMEM((4, nz, 32, 128), F32),
            dma((4, nz)),
            dma((4, nz)),
            dma((4, nz)),
            dma((4, nz)),
            dma,
            dma,
        ],
        compiler_params=pltpu.CompilerParams(collective_id=1, has_side_effects=True, vmem_limit_bytes=48 << 20),
        name="react",
    )(send, matrix)

    tile = sds((8, 8, 64))
    warm, salt, zonal, merid, final = plain(
        final_kernel, (tile, tile, tile, tile, sds((4, 512, 128))), name="final"
    )(adv, back, att, attp, ocean, tiles[4])
    warm, salt, zonal, merid = (jnp.transpose(a, (2, 0, 1)) for a in (warm, salt, zonal, merid))
    return warm, salt, zonal, merid, final.reshape(4, 64, 8, 128)


def solution(mesh):
    tile, tracers = P("lev", "cols", "trc"), P("trc", "lev", "cols", None)
    return jax.shard_map(
        functools.partial(shards, mesh.shape["trc"], mesh.shape["cols"]),
        mesh=mesh,
        in_specs=(tile, tile, tile, tile, tile, tracers, P(), P(), P()),
        out_specs=(tile, tile, tile, tile, tracers),
        check_vma=False,
    )
```

```python
import functools

import jax
import jax.numpy as jnp
from jax import lax
from jax.experimental import pallas as pl
from jax.experimental.pallas import tpu as pltpu
from jax.sharding import PartitionSpec as P

MESH = pl.DeviceIdType.MESH
F32 = jnp.float32
BF16 = jnp.bfloat16
I16 = jnp.int16
VMEM = pl.BlockSpec(memory_space=pltpu.VMEM)

viscosity = 0.2
buoyancy = 0.25
marine_advance = 0.05
tracer_step = 0.2
level_step = 0.04
react_step = 0.25
warming_amount = 60.0

LOW, AUX, HIGH = 0, 1024, 1152
BLOCK = 2176
PART = 1152


def sds(shape, dtype=F32):
    return jax.ShapeDtypeStruct(shape, dtype)


def iota(shape, axis):
    return lax.broadcasted_iota(jnp.int32, shape, axis)


def pieces(value):
    first = value.astype(BF16)
    rest = value - first.astype(F32)
    second = rest.astype(BF16)
    third = (rest - second.astype(F32)).astype(BF16)
    return first, second, third


def minmod_half(left, right):
    return jnp.maximum(jnp.minimum(left, right), jnp.minimum(jnp.maximum(left, right), 0.0))


def pack_kernel(t_ref, s_ref, u_ref, v_ref, m_ref, above_ref, sp_ref, b_ref, xs_ref):
    for f, ref in enumerate((t_ref, s_ref, u_ref, v_ref)):
        for k in range(4):
            off = (LOW if k < 2 else HIGH) + f * 256 + (k % 2) * 128
            b_ref[:, off : off + 128] = jnp.concatenate([ref[2 * k], ref[2 * k + 1]], axis=1)
    lane = iota((8, 128), 1)
    aux = above_ref[...]
    for x in range(8):
        count = jnp.sum(m_ref[x].astype(F32), axis=1, keepdims=True)
        aux = aux + jnp.where(lane == x, count, 0.0)
    b_ref[:, AUX : AUX + 128] = aux

    def one(t, carry):
        for x in range(8):
            xs_ref[t, x] = sp_ref[t, pl.ds(x, 64, stride=8), :]
        return carry

    lax.fori_loop(0, 4, one, 0)


def gather_kernel(nz, nx, b_ref, xs_ref, g_ref, gl_ref, gh_ref, se_ref, zs, zr, ls, lr, hs, hr, ss, sr):
    z, x, lev = lax.axis_index("trc"), lax.axis_index("cols"), lax.axis_index("lev")
    zup, zdn = {"trc": (z + 1) % nz}, {"trc": (z + nz - 1) % nz}
    xup, xdn = {"cols": (x + 1) % nx}, {"cols": (x + nx - 1) % nx}
    peer = {"lev": 1 - lev}
    barrier = pltpu.get_barrier_semaphore()
    for other in (zup, zdn, xup, xdn, peer):
        pl.semaphore_signal(barrier, inc=1, device_id=other, device_id_type=MESH)
    pl.semaphore_wait(barrier, 5)

    def rdma(src, dst, send, recv, to):
        return pltpu.make_async_remote_copy(
            src_ref=src, dst_ref=dst, send_sem=send, recv_sem=recv, device_id=to, device_id_type=MESH
        )

    def along(src, source, way):
        return rdma(src, g_ref.at[source], zs.at[way, source], zr.at[source], zup if way == 0 else zdn)

    def to_right(src, source):
        return rdma(src.at[:, AUX:], gl_ref.at[source], ls.at[source], lr.at[source], xup)

    def to_left(src, source):
        return rdma(src.at[:, :PART], gh_ref.at[source], hs.at[source], hr.at[source], xdn)

    along(b_ref, z, 0).start()
    along(b_ref, z, 1).start()
    to_right(b_ref, z).start()
    to_left(b_ref, z).start()

    near = pl.multiple_of((1 - lev) * 56, 8)
    there = pl.multiple_of((1 - lev) * 0 + lev * 72, 8)
    nothing = pl.multiple_of(lev * 72, 8)
    own_x = rdma(xs_ref.at[:, 4:8], se_ref.at[:, 0:4, 8:72], ss.at[0], sr.at[0], xup)
    own_y = rdma(xs_ref.at[:, 0:4], se_ref.at[:, 12:16, 8:72], ss.at[1], sr.at[1], xdn)
    own_l = rdma(xs_ref.at[:, :, pl.ds(near, 8)], se_ref.at[:, 4:12, pl.ds(there, 8)], ss.at[2], sr.at[2], peer)
    own_x.start()
    own_y.start()
    own_l.start()

    g_ref[z] = b_ref[...]

    def keep(t, carry):
        se_ref[t, 4:12, 8:72, :] = xs_ref[t]
        se_ref[t, :, pl.ds(nothing, 8), :] = jnp.zeros((16, 8, 128), F32)
        return carry

    lax.fori_loop(0, 4, keep, 0)

    near_e = pl.multiple_of(near + 8, 8)
    low_l = rdma(se_ref.at[:, 0:4, pl.ds(near_e, 8)], se_ref.at[:, 0:4, pl.ds(there, 8)], ss.at[3], sr.at[3], peer)
    high_l = rdma(se_ref.at[:, 12:16, pl.ds(near_e, 8)], se_ref.at[:, 12:16, pl.ds(there, 8)], ss.at[4], sr.at[4], peer)

    half = nz // 2
    for step in range(1, half + 1):
        source = (z + nz - step) % nz
        block = g_ref.at[source]
        along(block, source, 0).wait_recv()
        if step < half:
            along(block, source, 0).start()
        to_right(block, source).start()
        to_left(block, source).start()
        if step < half:
            source = (z + step) % nz
            block = g_ref.at[source]
            along(block, source, 1).wait_recv()
            if step < half - 1:
                along(block, source, 1).start()
            to_right(block, source).start()
            to_left(block, source).start()
        if step == half // 2:
            own_x.wait_recv()
            low_l.start()
            own_y.wait_recv()
            high_l.start()

    own_l.wait_recv()
    low_l.wait_recv()
    high_l.wait_recv()

    def arrived(source, carry):
        to_right(b_ref, source).wait_recv()
        to_left(b_ref, source).wait_recv()
        to_right(b_ref, source).wait_send()
        to_left(b_ref, source).wait_send()
        return carry

    lax.fori_loop(0, nz, arrived, 0)
    for step in range(half):
        along(b_ref, (z + nz - step) % nz, 0).wait_send()
    for step in range(half - 1):
        along(b_ref, (z + step) % nz, 1).wait_send()
    for copy in (own_x, own_y, own_l, low_l, high_l):
        copy.wait_send()


def flow_kernel(g_ref, gl_ref, gh_ref, uf_ref, vf_ref, fv_ref, t_ref, s_ref, bnd_ref, rho, uu, vv, pp, cnt, top):
    lev = lax.axis_index("lev")
    fields = (t_ref, s_ref, uu, vv)
    sides = ((gl_ref, 128), (g_ref, LOW), (g_ref, HIGH), (gh_ref, 0))
    for part, (ref, base) in enumerate(sides):
        for f, out in enumerate(fields):
            for k in range(2):
                off = base + f * 256 + k * 128
                r = part * 4 + k * 2
                out[r : r + 2] = ref[:, off : off + 128].T.reshape(2, 64, 128)
    aux, aux_l, aux_h = g_ref[:, AUX:HIGH].T, gl_ref[:, 0:128].T, gh_ref[:, AUX:HIGH].T
    cnt[0:4], cnt[4:12], cnt[12:16] = aux_l[4:8], aux[0:8], aux_h[0:4]
    top[0:4], top[4:12], top[12:16] = aux_l[12:16], aux[8:16], aux_h[8:12]

    row, col = iota((64, 64), 0), iota((64, 64), 1)
    down = jnp.where(col < row, 1.0, jnp.where(col == row, 0.5, 0.0)).astype(BF16)
    down = jnp.concatenate([down] * 3, axis=1)
    deep = jnp.where(col >= row, 1.0, 0.0).astype(BF16)
    deep = jnp.concatenate([deep] * 3, axis=1)
    for r in range(16):
        dense = 0.8 * s_ref[r] - 0.2 * t_ref[r]
        total = jnp.dot(down, jnp.concatenate(pieces(dense), axis=0), preferred_element_type=F32)
        pp[r] = buoyancy * (top[r : r + 1] + total)

    level = iota((64, 128), 0).astype(F32)
    uf_ref[0] = jnp.zeros((64, 128), F32)
    vf_ref[0] = jnp.zeros((64, 128), F32)
    for r in (14, 15):
        uf_ref[r] = jnp.zeros((64, 128), F32)
        vf_ref[r] = jnp.zeros((64, 128), F32)
    for r in range(1, 14):
        here, east = cnt[r : r + 1], cnt[r + 1 : r + 2]
        north = pltpu.roll(jnp.broadcast_to(here, (8, 128)), 127, 1)[0:1]
        p, u, v = pp[r], uu[r], vv[r]
        lap_u = uu[r + 1] + uu[r - 1] + pltpu.roll(u, 127, 1) + pltpu.roll(u, 1, 1) - 4.0 * u
        lap_v = vv[r + 1] + vv[r - 1] + pltpu.roll(v, 127, 1) + pltpu.roll(v, 1, 1) - 4.0 * v
        new_u = u + marine_advance * (p - pp[r + 1] + viscosity * lap_u)
        new_v = v + marine_advance * (p - pltpu.roll(p, 127, 1) + viscosity * lap_v)
        uf_ref[r] = jnp.where(level < jnp.minimum(here, east), new_u, 0.0)
        vf_ref[r] = jnp.where(level < jnp.minimum(here, north), new_v, 0.0)

    zero = jnp.zeros((1, 128), F32)
    first = lev == 0
    for r in range(16):
        if 2 <= r < 14:
            u, v = uf_ref[r], vf_ref[r]
            div = u - uf_ref[r - 1] + v - pltpu.roll(v, 1, 1)
            fv = jnp.dot(deep, jnp.concatenate(pieces(div), axis=0), preferred_element_type=F32)
            fv_ref[r] = fv
            flow = fv[0:1]
        else:
            fv_ref[r] = jnp.zeros((64, 128), F32)
            flow = zero
        u2 = jnp.where(first, uf_ref[r, 62:64], uf_ref[r, 0:2])
        v2 = jnp.where(first, vf_ref[r, 62:64], vf_ref[r, 0:2])
        t1 = jnp.where(first, t_ref[r, 63:64], t_ref[r, 0:1])
        s1 = jnp.where(first, s_ref[r, 63:64], s_ref[r, 0:1])
        bnd_ref[r] = jnp.concatenate([u2, v2, flow, t1, s1, zero], axis=0)


def matrix_kernel(c_ref, absorb_ref, w_ref):
    place, across = iota((512, 64), 0), iota((64, 512), 1)
    spread = jnp.where(place // 8 % 16 * 4 + place // 128 == iota((512, 64), 1), 1.0, 0.0).astype(BF16)
    across = jnp.where(across // 8 % 16 * 4 + across // 128 == iota((64, 512), 0), 1.0, 0.0).astype(BF16)
    tall = jnp.dot(spread, c_ref[...], preferred_element_type=F32).astype(BF16)
    wide = jnp.dot(tall, across, preferred_element_type=F32)
    w_ref[0:512] = jnp.where(iota((512, 512), 0) % 8 == iota((512, 512), 1) % 8, wide, 0.0).astype(BF16)
    own = iota((8, 512), 0) == iota((8, 512), 1) % 8
    rows = []
    for part in pieces(absorb_ref[...]):
        line = jnp.dot(part, across, preferred_element_type=F32)
        rows.append(jnp.where(own, line, 0.0))
    rows.append(jnp.zeros((8, 512), F32))
    w_ref[512:544] = jnp.concatenate(rows, axis=0).astype(BF16)


def react_kernel(
    nz, uf_ref, vf_ref, fv_ref, t_ref, s_ref, edge_ref, se_ref, w_ref,
    adv_ref, back_ref, scale_ref, att_ref, attp_ref, oc_ref,
    up, um, vp, vm, fp, fm, q1, ex, tr, bnd_ref, send_ref, got, res, sizes,
    s1, r1, s2, r2, s3, r3, s4, r4,
):
    z, lev = lax.axis_index("trc"), lax.axis_index("lev")
    first = lev == 0
    sub = iota((8, 128), 0)
    peer = {"lev": 1 - lev}
    barrier = pltpu.get_barrier_semaphore()

    def greet(d, carry):
        pl.semaphore_signal(barrier, inc=1, device_id={"trc": (z + d) % nz}, device_id_type=MESH)
        return carry

    lax.fori_loop(1, nz, greet, 0)
    pl.semaphore_signal(barrier, inc=1, device_id=peer, device_id_type=MESH)
    pl.semaphore_wait(barrier, nz)

    def rdma(src, dst, send, recv, to):
        return pltpu.make_async_remote_copy(
            src_ref=src, dst_ref=dst, send_sem=send, recv_sem=recv, device_id=to, device_id_type=MESH
        )

    def each(body):
        lax.fori_loop(1, nz, lambda d, carry: (body((z + d) % nz), carry)[1], 0)

    def out(t, to, at):
        return rdma(send_ref.at[t, to], got.at[t, at], s1.at[t, to], r1.at[t, at], {"trc": to})

    def home(c, to, at):
        return rdma(res.at[c, :, to], back_ref.at[c, :, at], s2.at[c, to], r2.at[c, at], {"trc": to})

    def size(c, to, at):
        return rdma(sizes.at[c, to], scale_ref.at[c, at], s4.at[c, to], r4.at[c, at], {"trc": to})

    edges = rdma(edge_ref.at[1:14], bnd_ref.at[1:14], s3.at[0], r3.at[0], peer)
    edges.start()
    mine = pl.multiple_of(z * 8, 8)
    for f, ref in enumerate((uf_ref, vf_ref)):
        for k in range(4):
            tr[...] = ref[4 + 2 * k : 6 + 2 * k].reshape(128, 128).T
            oc_ref[2 + f, :, k * 128 : k * 128 + 128] = tr[pl.ds(mine, 8), :]
    bnd_ref[0] = jnp.zeros((8, 128), F32)
    edges.wait_recv()

    def around(own, above, below):
        return jnp.concatenate(
            [jnp.where(first, 0.0, above), own, jnp.where(first, below, 0.0)], axis=0
        )

    def faces(r, carry):
        edge = bnd_ref[r]
        edge_w = bnd_ref[r - 1]
        pos = pltpu.roll(edge, 6, 0)
        u_ext = around(uf_ref[r], jnp.where(sub >= 6, pos, 0.0), jnp.where(sub < 2, edge, 0.0))
        two = pltpu.roll(edge, 4, 0)
        low = pltpu.roll(edge, 6, 0)
        v_ext = around(vf_ref[r], jnp.where(sub >= 6, two, 0.0), jnp.where(sub < 2, low, 0.0))
        d2 = edge[0:2] - edge_w[0:2] + edge[2:4] - pltpu.roll(edge, 1, 1)[2:4]
        d0, d1 = d2[0:1], d2[1:2]
        flow = jnp.where(first, edge[4:5], 0.0)
        f_own = fv_ref[r] + flow
        above = jnp.where(sub == 7, f_own[0:1] + d1, jnp.where(sub == 6, f_own[0:1] + d1 + d0, 0.0))
        below = jnp.where(
            sub == 0, flow, jnp.where(sub == 1, flow - d0, jnp.where(sub == 2, flow - d0 - d1, 0.0))
        )
        surface = jnp.where((iota((64, 128), 0) == 0) & first, 0.0, f_own)
        f_ext = level_step * around(surface, above, below)
        u_ext = tracer_step * u_ext
        v_ext = tracer_step * v_ext
        up[r], um[r] = jnp.maximum(u_ext, 0.0), jnp.minimum(u_ext, 0.0)
        vp[r], vm[r] = jnp.maximum(v_ext, 0.0), jnp.minimum(v_ext, 0.0)
        fp[r], fm[r] = jnp.maximum(f_ext, 0.0), jnp.minimum(f_ext, 0.0)
        return carry

    lax.fori_loop(1, 14, faces, 0)

    def sweep(load, store, start, stop):
        d_a = 0.5 * (load(start - 1) - load(start - 2))
        d_b = 0.5 * (load(start) - load(start - 1))
        d_c = 0.5 * (load(start + 1) - load(start))
        right = load(start - 1) + minmod_half(d_a, d_b)
        slope = minmod_half(d_b, d_c)
        flux = up[start - 1] * right + um[start - 1] * (load(start) - slope)

        def one(r, carry):
            d_here, right, flux = carry
            q, q_e = load(r), load(r + 1)
            d_next = 0.5 * (load(r + 2) - q_e)
            slope = minmod_half(d_here, d_next)
            flux_e = up[r] * right + um[r] * (q_e - slope)
            change = flux_e - flux
            right_e = q_e + slope
            north = 0.5 * (pltpu.roll(q, 127, 1) - q)
            slope = minmod_half(pltpu.roll(north, 1, 1), north)
            flux_n = vp[r] * (q + slope) + vm[r] * pltpu.roll(q - slope, 127, 1)
            change = change + (flux_n - pltpu.roll(flux_n, 1, 1))
            below = 0.5 * (pltpu.roll(q, 79, 0) - q)
            slope = minmod_half(pltpu.roll(below, 1, 0), below)
            flux_v = fp[r] * pltpu.roll(q + slope, 1, 0) + fm[r] * (q - slope)
            change = change + (pltpu.roll(flux_v, 79, 0) - flux_v)
            store(r, q - change)
            return d_next, right_e, flux_e

        lax.fori_loop(start, stop, one, (d_c, load(start) + slope, flux))

    def tracer(t, carry):
        def first_load(r):
            return se_ref[t, r]

        def first_store(r, value):
            q1[r] = value

        def second_load(r):
            return q1[r]

        def second_store(r, value):
            adv_ref[t, r - 4] = value[8:72]

        sweep(first_load, first_store, 2, 14)
        sweep(second_load, second_store, 4, 12)
        for k in range(4):
            across = adv_ref[t, 2 * k : 2 * k + 2].reshape(128, 128).T.reshape(16, 8, 128)
            send_ref[t, :, :, k * 128 : k * 128 + 128] = across.astype(BF16)
        each(lambda to: out(t, to, z).start())
        got[t, z] = send_ref[t, z]
        return carry

    lax.fori_loop(0, 4, tracer, 0)

    for f, ref in enumerate((t_ref, s_ref)):
        for r in range(3, 13):
            edge = bnd_ref[r][5 + f : 6 + f]
            ex[r] = around(ref[r], jnp.where(sub == 7, edge, 0.0), jnp.where(sub == 0, edge, 0.0))

        def donor(r, flux_w):
            c = ex[r]
            flux = up[r] * c + um[r] * ex[r + 1]
            flux_n = vp[r] * c + vm[r] * pltpu.roll(c, 127, 1)
            flux_v = fp[r] * pltpu.roll(c, 1, 0) + fm[r] * c
            wide = flux - flux_w + (flux_n - pltpu.roll(flux_n, 1, 1))
            tall = pltpu.roll(flux_v, 79, 0) - flux_v
            new = c - (marine_advance / tracer_step) * wide - (marine_advance / level_step) * tall
            q1[r] = new
            return flux

        lax.fori_loop(4, 12, donor, up[3] * ex[3] + um[3] * ex[4])
        for k in range(4):
            both = jnp.concatenate([q1[4 + 2 * k, 8:72], q1[5 + 2 * k, 8:72]], axis=0)
            tr[...] = both.T
            oc_ref[f, :, k * 128 : k * 128 + 128] = tr[pl.ds(mine, 8), :]

    lax.fori_loop(0, 4, lambda t, carry: (each(lambda at: out(t, at, at).wait_recv()), carry)[1], 0)
    for c in range(4):
        values = got[:, :, :, c * 128 : c * 128 + 128].reshape(512, 128)
        values = jnp.dot(w_ref[...], values, preferred_element_type=F32)
        att_ref[c] = values[512:520] + values[520:528] + values[528:536]
        values = values[0:512].reshape(4, nz, 8, 128)
        largest = jnp.max(jnp.max(jnp.abs(values), axis=0), axis=1, keepdims=True)
        largest = jnp.maximum(largest, 1e-30)
        sizes[c] = largest * (1.0 / 32767.0)
        coded = jnp.round(values * (32767.0 / largest)[None])
        res[c] = coded.astype(jnp.int32).astype(I16)
        each(lambda to: (home(c, to, z).start(), size(c, to, z).start()))
        back_ref[c, :, z] = res[c, :, z]
        scale_ref[c, z] = sizes[c, z]
    shade = rdma(att_ref, attp_ref, s3.at[1], r3.at[1], peer)
    shade.start()
    for c in range(4):

        def finish(at):
            home(c, at, at).wait_recv()
            size(c, at, at).wait_recv()
            out(c, at, at).wait_send()
            home(c, at, at).wait_send()
            size(c, at, at).wait_send()

        each(finish)
    shade.wait_recv()
    shade.wait_send()
    edges.wait_send()


def final_kernel(adv_ref, back_ref, scale_ref, att_ref, attp_ref, oc_ref, m_ref, w_ref, s_ref, u_ref, v_ref, sp_ref):
    lev = lax.axis_index("lev")

    def one(t, carry):
        for c in range(4):
            react = back_ref[c, t].astype(jnp.int32).astype(F32) * scale_ref[c]
            react = react.reshape(128, 128).T
            new = adv_ref[t, 2 * c : 2 * c + 2].reshape(128, 128) + react_step * react
            sp_ref[t, pl.ds(2 * c, 64, stride=8), :] = new[0:64]
            sp_ref[t, pl.ds(2 * c + 1, 64, stride=8), :] = new[64:128]
        return carry

    lax.fori_loop(0, 4, one, 0)
    row, col = iota((128, 128), 0), iota((128, 128), 1)
    same = row // 64 == col // 64
    before = jnp.where(same & (row < col), 1.0, 0.0).astype(BF16)
    every = jnp.where(same & (lev == 1), 1.0, 0.0).astype(BF16)
    sums = jnp.concatenate([before] * 3 + [every] * 3, axis=0)
    for c in range(4):
        att = att_ref[c]
        terms = jnp.concatenate(pieces(att) + pieces(attp_ref[c]), axis=1)
        path = jnp.dot(terms, sums, preferred_element_type=F32)
        caught = jnp.exp(-path) * (1.0 - jnp.exp(-att))
        wet = jnp.concatenate([m_ref[2 * c], m_ref[2 * c + 1]], axis=1).astype(F32)
        lanes = slice(c * 128, c * 128 + 128)
        warm = oc_ref[0, :, lanes] + warming_amount * wet * caught
        for out, value in ((w_ref, warm), (s_ref, oc_ref[1, :, lanes]), (u_ref, oc_ref[2, :, lanes]), (v_ref, oc_ref[3, :, lanes])):
            out[2 * c] = value[:, 0:64]
            out[2 * c + 1] = value[:, 64:128]


def plain(kernel, outs, scratch=(), name=None):
    return pl.pallas_call(
        kernel,
        out_shape=outs,
        out_specs=jax.tree.map(lambda _: VMEM, outs),
        scratch_shapes=list(scratch),
        compiler_params=pltpu.CompilerParams(vmem_limit_bytes=48 << 20),
        name=name,
    )


def shards(
    nz,
    nx,
    potential_warmth,
    saltiness_anomaly,
    zonal_speed,
    meridional_speed,
    marine_indicator,
    species_concentrations,
    coupling_matrix,
    species_guild_number,
    guild_extinction_coefficient,
):
    tiles = [
        jnp.transpose(a, (1, 2, 0))
        for a in (potential_warmth, saltiness_anomaly, zonal_speed, meridional_speed, marine_indicator)
    ]
    dense = jnp.sum(0.8 * tiles[1] - 0.2 * tiles[0], axis=2)
    above = lax.ppermute(dense, "lev", [(0, 1)])
    above = jnp.pad(above.T, ((0, 0), (8, 112)))
    species = species_concentrations.reshape(4, 512, 128)
    block, xs = plain(pack_kernel, (sds((8, BLOCK)), sds((4, 8, 64, 128))), name="pack")(*tiles, above, species)

    dma = pltpu.SemaphoreType.DMA
    gathered, left, right, ext = pl.pallas_call(
        functools.partial(gather_kernel, nz, nx),
        out_shape=(sds((nz, 8, BLOCK)), sds((nz, 8, PART)), sds((nz, 8, PART)), sds((4, 16, 80, 128))),
        in_specs=[VMEM] * 2,
        out_specs=(VMEM,) * 4,
        scratch_shapes=[dma((2, nz)), dma((nz,)), dma((nz,)), dma((nz,)), dma((nz,)), dma((nz,)), dma((5,)), dma((5,))],
        compiler_params=pltpu.CompilerParams(collective_id=0, has_side_effects=True, vmem_limit_bytes=48 << 20),
        name="gather",
    )(block, xs)

    row = sds((16, 64, 128))
    big = pltpu.VMEM((16, 64, 128), F32)
    small = pltpu.VMEM((16, 128), F32)
    uf, vf, fv, t_ext, s_ext, edge = plain(
        flow_kernel, (row, row, row, row, row, sds((16, 8, 128))), [big, big, big, big, small, small], name="flow"
    )(gathered.reshape(128, BLOCK), left.reshape(128, PART), right.reshape(128, PART))
    onehot = species_guild_number[None, :] == lax.broadcasted_iota(jnp.int32, (8, 64), 0)
    absorb = jnp.sum(jnp.where(onehot, guild_extinction_coefficient[:, None], 0.0), axis=0, keepdims=True)
    absorb = jnp.broadcast_to(absorb, (8, 64))
    matrix = plain(matrix_kernel, sds((544, 512), BF16), name="matrix")(coupling_matrix, absorb)

    tall = pltpu.VMEM((16, 80, 128), F32)
    adv, back, scale, att, attp, ocean = pl.pallas_call(
        functools.partial(react_kernel, nz),
        out_shape=(
            sds((4, 8, 64, 128)),
            sds((4, 4, nz, 8, 128), I16),
            sds((4, nz, 1, 128)),
            sds((4, 8, 128)),
            sds((4, 8, 128)),
            sds((4, 8, 512)),
        ),
        in_specs=[VMEM] * 8,
        out_specs=(VMEM,) * 6,
        scratch_shapes=[tall] * 8
        + [
            pltpu.VMEM((128, 128), F32),
            pltpu.VMEM((16, 8, 128), F32),
            pltpu.VMEM((4, nz, 8, 512), BF16),
            pltpu.VMEM((4, nz, 8, 512), BF16),
            pltpu.VMEM((4, 4, nz, 8, 128), I16),
            pltpu.VMEM((4, nz, 1, 128), F32),
        ]
        + [dma((4, nz))] * 4
        + [dma((2,))] * 2
        + [dma((4, nz))] * 2,
        compiler_params=pltpu.CompilerParams(collective_id=1, has_side_effects=True, vmem_limit_bytes=48 << 20),
        name="react",
    )(uf, vf, fv, t_ext, s_ext, edge, ext, matrix)

    tile = sds((8, 8, 64))
    warm, salt, zonal, merid, final = plain(
        final_kernel, (tile, tile, tile, tile, sds((4, 512, 128))), name="final"
    )(adv, back, scale, att, attp, ocean, tiles[4])
    warm, salt, zonal, merid = (jnp.transpose(a, (2, 0, 1)) for a in (warm, salt, zonal, merid))
    return warm, salt, zonal, merid, final.reshape(4, 64, 8, 128)


def solution(mesh):
    tile, tracers = P("lev", "cols", "trc"), P("trc", "lev", "cols", None)
    return jax.shard_map(
        functools.partial(shards, mesh.shape["trc"], mesh.shape["cols"]),
        mesh=mesh,
        in_specs=(tile, tile, tile, tile, tile, tracers, P(), P(), P()),
        out_specs=(tile, tile, tile, tile, tracers),
        check_vma=False,
    )
```

```python
import functools

import jax
import jax.numpy as jnp
from jax import lax
from jax.experimental import pallas as pl
from jax.experimental.pallas import tpu as pltpu
from jax.sharding import PartitionSpec as P

MESH = pl.DeviceIdType.MESH
F32 = jnp.float32
BF16 = jnp.bfloat16
I16 = jnp.int16

viscosity = 0.2
buoyancy = 0.25
marine_advance = 0.05
tracer_step = 0.2
level_step = 0.04
react_step = 0.25
warming_amount = 60.0

SPEEDS, WATER = 1024, 1152


def sds(shape, dtype=F32):
    return jax.ShapeDtypeStruct(shape, dtype)


def iota(shape, axis):
    return lax.broadcasted_iota(jnp.int32, shape, axis)


def pieces(value):
    first = value.astype(BF16)
    rest = value - first.astype(F32)
    second = rest.astype(BF16)
    third = (rest - second.astype(F32)).astype(BF16)
    return first, second, third


def minmod_half(left, right):
    return jnp.maximum(jnp.minimum(left, right), jnp.minimum(jnp.maximum(left, right), 0.0))


def gather_kernel(
    nz, nx, t_hbm, s_hbm, u_hbm, v_hbm, m_hbm, sp_hbm,
    ga, gb, la, lb, ha, hb, se,
    t_in, s_in, u_in, v_in, m_in, sp_in, a_own, b_own, d_own, d_peer,
    ins, zs, zr, ls, lr, hs, hr, ss, sr,
):
    z, x, lev = lax.axis_index("trc"), lax.axis_index("cols"), lax.axis_index("lev")
    zup, zdn = {"trc": (z + 1) % nz}, {"trc": (z + nz - 1) % nz}
    xup, xdn = {"cols": (x + 1) % nx}, {"cols": (x + nx - 1) % nx}
    peer = {"lev": 1 - lev}
    loads = [
        pltpu.make_async_copy(src, dst, ins.at[i])
        for i, (src, dst) in enumerate(
            ((u_hbm, u_in), (v_hbm, v_in), (t_hbm, t_in), (s_hbm, s_in), (m_hbm, m_in), (sp_hbm, sp_in))
        )
    ]
    for load in loads:
        load.start()
    barrier = pltpu.get_barrier_semaphore()
    for other in (xup, xdn, peer):
        pl.semaphore_signal(barrier, inc=1, device_id=other, device_id_type=MESH)

    def greet(d, carry):
        pl.semaphore_signal(barrier, inc=1, device_id={"trc": (z + d) % nz}, device_id_type=MESH)
        return carry

    lax.fori_loop(1, nz, greet, 0)

    def rdma(src, dst, send, recv, to):
        return pltpu.make_async_remote_copy(
            src_ref=src, dst_ref=dst, send_sem=send, recv_sem=recv, device_id=to, device_id_type=MESH
        )

    wholes, lefts, rights = (ga, gb), (la, lb), (ha, hb)
    upper, lower = (SPEEDS // 2, 512), (SPEEDS // 2, 640)

    def along(k, src, source, way):
        return rdma(src, wholes[k].at[source], zs.at[k, way, source], zr.at[k, source], zup if way == 0 else zdn)

    def to_right(k, src, source):
        return rdma(src.at[:, upper[k] :], lefts[k].at[source], ls.at[k, source], lr.at[k, source], xup)

    def to_left(k, src, source):
        return rdma(src.at[:, : lower[k]], rights[k].at[source], hs.at[k, source], hr.at[k, source], xdn)

    def fill(block, refs, high):
        for f, ref in enumerate(refs):
            for k in range(4):
                off = (0 if k < 2 else high) + f * 256 + (k % 2) * 128
                block[:, off : off + 128] = jnp.concatenate([ref[2 * k], ref[2 * k + 1]], axis=1)

    def begin(k, block):
        along(k, block, z, 0).start()
        along(k, block, z, 1).start()
        to_right(k, block, z).start()
        to_left(k, block, z).start()
        wholes[k][z] = block[...]

    loads[0].wait()
    loads[1].wait()
    fill(a_own, (u_in, v_in), 512)
    pl.semaphore_wait(barrier, nz + 2)
    begin(0, a_own)

    for load in loads[2:5]:
        load.wait()
    lane = iota((8, 128), 1)
    counts = jnp.zeros((8, 128), F32)
    dense = jnp.zeros((8, 128), F32)
    for i in range(8):
        counts = counts + jnp.where(lane == i, jnp.sum(m_in[i].astype(F32), axis=1, keepdims=True), 0.0)
        column = jnp.sum(0.8 * s_in[i] - 0.2 * t_in[i], axis=1, keepdims=True)
        dense = dense + jnp.where(lane == i + 8, column, 0.0)
    d_own[...] = dense
    above = rdma(d_own, d_peer, ss.at[5], sr.at[5], peer)
    above.start()
    fill(b_own, (t_in, s_in), 640)

    loads[5].wait()

    def spread(t, carry):
        for i in range(8):
            se[t, 4 + i, 8:72, :] = sp_in[t, pl.ds(i, 64, stride=8), :]
        return carry

    lax.fori_loop(0, 4, spread, 0)
    near = pl.multiple_of((1 - lev) * 56 + 8, 8)
    there = pl.multiple_of(lev * 72, 8)
    own_x = rdma(se.at[:, 8:12, 8:72], se.at[:, 0:4, 8:72], ss.at[0], sr.at[0], xup)
    own_y = rdma(se.at[:, 4:8, 8:72], se.at[:, 12:16, 8:72], ss.at[1], sr.at[1], xdn)
    parts = [
        rdma(se.at[:, low:high, pl.ds(near, 8)], se.at[:, low:high, pl.ds(there, 8)], ss.at[i], sr.at[i], peer)
        for i, low, high in ((2, 4, 12), (3, 0, 4), (4, 12, 16))
    ]
    above.wait_recv()
    b_own[:, 512:640] = counts + jnp.where(lev == 1, d_peer[...], 0.0)
    begin(1, b_own)
    own_x.start()
    own_y.start()
    parts[0].start()

    def clear(t, carry):
        se[t, :, pl.ds(there, 8), :] = jnp.zeros((16, 8, 128), F32)
        return carry

    lax.fori_loop(0, 4, clear, 0)
    half = nz // 2
    for step in range(1, half + 1):
        came = []
        for k in range(2):
            for way, source in ((0, (z + nz - step) % nz), (1, (z + step) % nz))[: 2 if step < half else 1]:
                block = wholes[k].at[source]
                along(k, block, source, way).wait_recv()
                if step < half - way:
                    along(k, block, source, way).start()
                came.append((k, block, source))
        for k, block, source in came:
            to_right(k, block, source).start()
            to_left(k, block, source).start()
        if step == 3:
            own_x.wait_recv()
            parts[1].start()
            own_y.wait_recv()
            parts[2].start()

    for part in parts:
        part.wait_recv()
        part.wait_send()

    for k, block in ((0, a_own), (1, b_own)):

        def arrived(source, carry):
            to_right(k, block, source).wait_recv()
            to_left(k, block, source).wait_recv()
            to_right(k, block, source).wait_send()
            to_left(k, block, source).wait_send()
            return carry

        lax.fori_loop(0, nz, arrived, 0)
        for step in range(half):
            along(k, block, (z + nz - step) % nz, 0).wait_send()
        for step in range(half - 1):
            along(k, block, (z + step) % nz, 1).wait_send()
    for copy in (own_x, own_y, above):
        copy.wait_send()


def flow_kernel(ga, gb, la, lb, ha, hb, uf_ref, vf_ref, fv_ref, t_ref, s_ref, bnd_ref, uu, vv, pp, cnt, top):
    lev = lax.axis_index("lev")
    sides = (
        ((uu, vv), ((la, 0), (ga, 0), (ga, 512), (ha, 0))),
        ((t_ref, s_ref), ((lb, 128), (gb, 0), (gb, 640), (hb, 0))),
    )
    for fields, sources in sides:
        for part, (ref, base) in enumerate(sources):
            for f, out in enumerate(fields):
                for k in range(2):
                    off = base + f * 256 + k * 128
                    r = part * 4 + k * 2
                    out[r : r + 2] = ref[:, :, off : off + 128].reshape(128, 128).T.reshape(2, 64, 128)
    aux = gb[:, :, 512:640].reshape(128, 128).T
    aux_l = lb[:, :, 0:128].reshape(128, 128).T
    aux_h = hb[:, :, 512:640].reshape(128, 128).T
    cnt[0:4], cnt[4:12], cnt[12:16] = aux_l[4:8], aux[0:8], aux_h[0:4]
    top[0:4], top[4:12], top[12:16] = aux_l[12:16], aux[8:16], aux_h[8:12]

    row, col = iota((64, 64), 0), iota((64, 64), 1)
    down = jnp.where(col < row, 1.0, jnp.where(col == row, 0.5, 0.0)).astype(BF16)
    down = jnp.concatenate([down] * 3, axis=1)
    deep = jnp.where(col >= row, 1.0, 0.0).astype(BF16)
    deep = jnp.concatenate([deep] * 3, axis=1)
    for r in range(16):
        dense = 0.8 * s_ref[r] - 0.2 * t_ref[r]
        total = jnp.dot(down, jnp.concatenate(pieces(dense), axis=0), preferred_element_type=F32)
        pp[r] = buoyancy * (top[r : r + 1] + total)

    level = iota((64, 128), 0).astype(F32)
    uf_ref[0] = jnp.zeros((64, 128), F32)
    vf_ref[0] = jnp.zeros((64, 128), F32)
    for r in (14, 15):
        uf_ref[r] = jnp.zeros((64, 128), F32)
        vf_ref[r] = jnp.zeros((64, 128), F32)
    for r in range(1, 14):
        here, east = cnt[r : r + 1], cnt[r + 1 : r + 2]
        north = pltpu.roll(jnp.broadcast_to(here, (8, 128)), 127, 1)[0:1]
        p, u, v = pp[r], uu[r], vv[r]
        lap_u = uu[r + 1] + uu[r - 1] + pltpu.roll(u, 127, 1) + pltpu.roll(u, 1, 1) - 4.0 * u
        lap_v = vv[r + 1] + vv[r - 1] + pltpu.roll(v, 127, 1) + pltpu.roll(v, 1, 1) - 4.0 * v
        new_u = u + marine_advance * (p - pp[r + 1] + viscosity * lap_u)
        new_v = v + marine_advance * (p - pltpu.roll(p, 127, 1) + viscosity * lap_v)
        uf_ref[r] = jnp.where(level < jnp.minimum(here, east), new_u, 0.0)
        vf_ref[r] = jnp.where(level < jnp.minimum(here, north), new_v, 0.0)

    zero = jnp.zeros((1, 128), F32)
    first = lev == 0
    for r in range(16):
        if 2 <= r < 14:
            u, v = uf_ref[r], vf_ref[r]
            div = u - uf_ref[r - 1] + v - pltpu.roll(v, 1, 1)
            fv = jnp.dot(deep, jnp.concatenate(pieces(div), axis=0), preferred_element_type=F32)
            fv_ref[r] = fv
            flow = fv[0:1]
        else:
            fv_ref[r] = jnp.zeros((64, 128), F32)
            flow = zero
        u2 = jnp.where(first, uf_ref[r, 62:64], uf_ref[r, 0:2])
        v2 = jnp.where(first, vf_ref[r, 62:64], vf_ref[r, 0:2])
        t1 = jnp.where(first, t_ref[r, 63:64], t_ref[r, 0:1])
        s1 = jnp.where(first, s_ref[r, 63:64], s_ref[r, 0:1])
        bnd_ref[r] = jnp.concatenate([u2, v2, flow, t1, s1, zero], axis=0)


def fill_matrix(c_ref, guild_ref, light_ref, w_ref):
    kinds = iota((8, 64), 0) == guild_ref[...]
    light = jnp.sum(jnp.where(iota((8, 8), 0) == iota((8, 8), 1), light_ref[...], 0.0), axis=1, keepdims=True)
    absorb = jnp.sum(jnp.where(kinds, light, 0.0), axis=0, keepdims=True)
    absorb = jnp.broadcast_to(absorb, (8, 64))
    place, across = iota((512, 64), 0), iota((64, 512), 1)
    spread = jnp.where(place // 8 % 16 * 4 + place // 128 == iota((512, 64), 1), 1.0, 0.0).astype(BF16)
    across = jnp.where(across // 8 % 16 * 4 + across // 128 == iota((64, 512), 0), 1.0, 0.0).astype(BF16)
    tall = jnp.dot(spread, c_ref[...], preferred_element_type=F32).astype(BF16)
    wide = jnp.dot(tall, across, preferred_element_type=F32)
    w_ref[0:512] = jnp.where(iota((512, 512), 0) % 8 == iota((512, 512), 1) % 8, wide, 0.0).astype(BF16)
    own = iota((8, 512), 0) == iota((8, 512), 1) % 8
    rows = []
    for part in pieces(absorb):
        line = jnp.dot(part, across, preferred_element_type=F32)
        rows.append(jnp.where(own, line, 0.0))
    rows.append(jnp.zeros((8, 512), F32))
    w_ref[512:544] = jnp.concatenate(rows, axis=0).astype(BF16)


def react_kernel(
    nz, uf_ref, vf_ref, fv_ref, t_ref, s_ref, edge_ref, se_ref, c_ref, guild_ref, light_ref,
    adv_ref, back_ref, scale_ref, att_ref, attp_ref, oc_ref, adv_out, att_out, oc_out, out_sems,
    up, um, vp, vm, fp, fm, q1, ex, tr, yd, vpt, vmt, vpu, vmu, rest, bnd_ref, w_ref, send_ref, got, res, sizes,
    s1, r1, s2, r2, s3, r3, s4, r4,
):
    z, lev = lax.axis_index("trc"), lax.axis_index("lev")
    first = lev == 0
    sub = iota((8, 128), 0)
    peer = {"lev": 1 - lev}
    def rdma(src, dst, send, recv, to):
        return pltpu.make_async_remote_copy(
            src_ref=src, dst_ref=dst, send_sem=send, recv_sem=recv, device_id=to, device_id_type=MESH
        )

    def each(body):
        def one(i, carry):
            d = nz // 2 + (i + 1) // 2 * (1 - i % 2 * 2)
            body((z + d) % nz)
            return carry

        lax.fori_loop(0, nz - 1, one, 0)

    def out(t, to, at):
        return rdma(send_ref.at[t, to], got.at[t, at], s1.at[t, to], r1.at[t, at], {"trc": to})

    def home(c, to, at):
        return rdma(res.at[c, :, to], back_ref.at[c, :, at], s2.at[c, to], r2.at[c, at], {"trc": to})

    def size(c, to, at):
        return rdma(sizes.at[c, to], scale_ref.at[c, at], s4.at[c, to], r4.at[c, at], {"trc": to})

    def stored(t):
        return pltpu.make_async_copy(adv_ref.at[t], adv_out.at[t], out_sems.at[t])

    def own_back(c):
        return pltpu.make_async_copy(res.at[c, :, z], back_ref.at[c, :, z], out_sems.at[4 + c])

    def own_scale(c):
        return pltpu.make_async_copy(sizes.at[c, z], scale_ref.at[c, z], out_sems.at[8 + c])

    ocean = pltpu.make_async_copy(oc_ref, oc_out, out_sems.at[12])
    shades = pltpu.make_async_copy(att_ref, att_out, out_sems.at[13])
    edges = rdma(edge_ref.at[1:14], bnd_ref.at[1:14], s3.at[0], r3.at[0], peer)
    edges.start()
    mine = pl.multiple_of(z * 8, 8)
    for f, ref in enumerate((uf_ref, vf_ref)):
        for k in range(4):
            tr[...] = ref[4 + 2 * k : 6 + 2 * k].reshape(128, 128).T
            oc_ref[2 + f, :, k * 128 : k * 128 + 128] = tr[pl.ds(mine, 8), :]
    fill_matrix(c_ref, guild_ref, light_ref, w_ref)
    bnd_ref[0] = jnp.zeros((8, 128), F32)
    edges.wait_recv()

    def rows(r):
        return pl.ds(pl.multiple_of(r * 80, 8), 80)

    def around(own, above, below):
        return jnp.concatenate(
            [jnp.where(first, 0.0, above), own, jnp.where(first, below, 0.0)], axis=0
        )

    def faces(r, carry):
        edge = bnd_ref[r]
        edge_w = bnd_ref[r - 1]
        pos = pltpu.roll(edge, 6, 0)
        u_ext = around(uf_ref[r], jnp.where(sub >= 6, pos, 0.0), jnp.where(sub < 2, edge, 0.0))
        two = pltpu.roll(edge, 4, 0)
        low = pltpu.roll(edge, 6, 0)
        v_ext = around(vf_ref[r], jnp.where(sub >= 6, two, 0.0), jnp.where(sub < 2, low, 0.0))
        d2 = edge[0:2] - edge_w[0:2] + edge[2:4] - pltpu.roll(edge, 1, 1)[2:4]
        d0, d1 = d2[0:1], d2[1:2]
        flow = jnp.where(first, edge[4:5], 0.0)
        f_own = fv_ref[r] + flow
        above = jnp.where(sub == 7, f_own[0:1] + d1, jnp.where(sub == 6, f_own[0:1] + d1 + d0, 0.0))
        below = jnp.where(
            sub == 0, flow, jnp.where(sub == 1, flow - d0, jnp.where(sub == 2, flow - d0 - d1, 0.0))
        )
        surface = jnp.where((iota((64, 128), 0) == 0) & first, 0.0, f_own)
        f_ext = level_step * around(surface, above, below)
        u_ext = tracer_step * u_ext
        v_ext = tracer_step * v_ext
        up[r], um[r] = jnp.maximum(u_ext, 0.0), jnp.minimum(u_ext, 0.0)
        vp[rows(r)], vm[rows(r)] = jnp.maximum(v_ext, 0.0), jnp.minimum(v_ext, 0.0)
        fp[r], fm[r] = jnp.maximum(f_ext, 0.0), jnp.minimum(f_ext, 0.0)
        return carry

    lax.fori_loop(1, 14, faces, 0)

    def turn_faces(ref, wide, narrow):
        for c in range(9):
            wide[c] = ref[64 + 128 * c : 192 + 128 * c].T
        for k in range(4):
            row = (4 + 2 * k) * 80 + 8
            both = jnp.concatenate([ref[row : row + 64], ref[row + 80 : row + 144]], axis=0)
            narrow[k] = both.T

    turn_faces(vp, vpt, vpu)
    turn_faces(vm, vmt, vmu)

    def along_y(q, plus, minus):
        north = 0.5 * (pltpu.roll(q, 127, 0) - q)
        slope = minmod_half(pltpu.roll(north, 1, 0), north)
        flux = plus * (q + slope) + minus * pltpu.roll(q - slope, 127, 0)
        return flux - pltpu.roll(flux, 1, 0)

    def sweep(load, store, start, stop):
        d_a = 0.5 * (load(start - 1) - load(start - 2))
        d_b = 0.5 * (load(start) - load(start - 1))
        d_c = 0.5 * (load(start + 1) - load(start))
        right = load(start - 1) + minmod_half(d_a, d_b)
        slope = minmod_half(d_b, d_c)
        flux = up[start - 1] * right + um[start - 1] * (load(start) - slope)

        def one(r, carry):
            d_here, right, flux = carry
            q, q_e = load(r), load(r + 1)
            d_next = 0.5 * (load(r + 2) - q_e)
            slope = minmod_half(d_here, d_next)
            flux_e = up[r] * right + um[r] * (q_e - slope)
            change = flux_e - flux
            right_e = q_e + slope
            below = 0.5 * (pltpu.roll(q, 79, 0) - q)
            slope = minmod_half(pltpu.roll(below, 1, 0), below)
            flux_v = fp[r] * pltpu.roll(q + slope, 1, 0) + fm[r] * (q - slope)
            change = change + (pltpu.roll(flux_v, 79, 0) - flux_v)
            store(r, q - change)
            return d_next, right_e, flux_e

        lax.fori_loop(start, stop, one, (d_c, load(start) + slope, flux))

    def tracer(t, carry):
        def first_load(r):
            return se_ref[t, r]

        def first_store(r, value):
            q1[rows(r)] = value - yd[rows(r)]

        def second_load(r):
            return q1[rows(r)]

        def second_store(r, value):
            rest[r - 4] = value[8:72]

        for c in range(9):
            start, stop = 64 + 128 * c, 192 + 128 * c
            q = [se_ref[t, r, max(start - r * 80, 0) : min(stop - r * 80, 80)] for r in range(start // 80, (stop + 79) // 80)]
            q = jnp.concatenate(q, axis=0).T
            yd[64 + 128 * c : 192 + 128 * c] = along_y(q, vpt[c], vmt[c]).T
        sweep(first_load, first_store, 2, 14)
        sweep(second_load, second_store, 4, 12)
        for k in range(4):
            row = (4 + 2 * k) * 80 + 8
            q = jnp.concatenate([q1[row : row + 64], q1[row + 80 : row + 144]], axis=0).T
            new = rest[2 * k : 2 * k + 2].reshape(128, 128).T - along_y(q, vpu[k], vmu[k])
            adv_ref[t, k] = new
            send_ref[t, :, :, k * 128 : k * 128 + 128] = new.reshape(16, 8, 128).astype(BF16)
        each(lambda to: out(t, to, z).start())
        got[t, z] = send_ref[t, z]
        stored(t).start()
        return carry

    lax.fori_loop(0, 4, tracer, 0)

    for f, ref in enumerate((t_ref, s_ref)):
        for r in range(3, 13):
            edge = bnd_ref[r][5 + f : 6 + f]
            ex[r] = around(ref[r], jnp.where(sub == 7, edge, 0.0), jnp.where(sub == 0, edge, 0.0))

        def donor(r, flux_w):
            c = ex[r]
            flux = up[r] * c + um[r] * ex[r + 1]
            flux_n = vp[rows(r)] * c + vm[rows(r)] * pltpu.roll(c, 127, 1)
            flux_v = fp[r] * pltpu.roll(c, 1, 0) + fm[r] * c
            wide = flux - flux_w + (flux_n - pltpu.roll(flux_n, 1, 1))
            tall = pltpu.roll(flux_v, 79, 0) - flux_v
            new = c - (marine_advance / tracer_step) * wide - (marine_advance / level_step) * tall
            q1[rows(r)] = new
            return flux

        lax.fori_loop(4, 12, donor, up[3] * ex[3] + um[3] * ex[4])
        for k in range(4):
            row = (4 + 2 * k) * 80 + 8
            both = jnp.concatenate([q1[row : row + 64], q1[row + 80 : row + 144]], axis=0)
            tr[...] = both.T
            oc_ref[f, :, k * 128 : k * 128 + 128] = tr[pl.ds(mine, 8), :]
    ocean.start()

    lax.fori_loop(0, 4, lambda t, carry: (each(lambda at: out(t, at, at).wait_recv()), carry)[1], 0)
    for c in range(4):
        values = got[:, :, :, c * 128 : c * 128 + 128].reshape(512, 128)
        values = jnp.dot(w_ref[...], values, preferred_element_type=F32)
        att_ref[c] = values[512:520] + values[520:528] + values[528:536]
        values = values[0:512].reshape(4, nz, 8, 128)
        largest = jnp.max(jnp.max(jnp.abs(values), axis=0), axis=1, keepdims=True)
        largest = jnp.maximum(largest, 1e-30)
        sizes[c] = largest * (1.0 / 32767.0)
        coded = jnp.round(values * (32767.0 / largest)[None])
        res[c] = coded.astype(jnp.int32).astype(I16)
        each(lambda to: (home(c, to, z).start(), size(c, to, z).start()))
        own_back(c).start()
        own_scale(c).start()
    shade = rdma(att_ref, attp_ref, s3.at[1], r3.at[1], peer)
    shade.start()
    shades.start()
    for c in range(4):

        def finish(at):
            home(c, at, at).wait_recv()
            size(c, at, at).wait_recv()
            out(c, at, at).wait_send()
            home(c, at, at).wait_send()
            size(c, at, at).wait_send()

        each(finish)
    shade.wait_recv()
    shade.wait_send()
    edges.wait_send()
    for c in range(4):
        stored(c).wait()
        own_back(c).wait()
        own_scale(c).wait()
    ocean.wait()
    shades.wait()


GATHERED = 7
LOADED = 10
ARRIVALS = 9
FLOWS = 6


def step_kernel(nz, nx, *refs):
    fields, params, outs, scratch = refs[:6], refs[6:9], refs[9:15], refs[15:]
    gathered, scratch = scratch[:GATHERED], scratch[GATHERED:]
    loaded, scratch = scratch[: LOADED + ARRIVALS], scratch[LOADED + ARRIVALS :]
    flows, scratch = scratch[:FLOWS], scratch[FLOWS:]
    temporary, scratch = scratch[:5], scratch[5:]
    held, scratch = scratch[:3], scratch[3:]
    param_sems, out_sems, adv_ref, att_ref, oc_ref = scratch[:5]
    loads = [pltpu.make_async_copy(src, dst, param_sems.at[i]) for i, (src, dst) in enumerate(zip(params, held))]
    for load in loads:
        load.start()
    gather_kernel(nz, nx, *fields, *gathered, *loaded)
    flow_kernel(*gathered[:6], *flows, *temporary)
    for load in loads:
        load.wait()
    adv_out, back_ref, scale_ref, att_out, attp_ref, oc_out = outs
    react_kernel(
        nz, *flows, gathered[6], *held, adv_ref, back_ref, scale_ref, att_ref, attp_ref, oc_ref,
        adv_out, att_out, oc_out, out_sems, *scratch[5:]
    )


def final_kernel(
    adv_hbm, back_hbm, scale_hbm, att_hbm, attp_hbm, oc_hbm, m_hbm,
    w_hbm, s_hbm, u_hbm, v_hbm, sp_hbm,
    adv_ref, back_ref, scale_ref, att_ref, attp_ref, oc_ref, m_ref, w_ref, s_ref, u_ref, v_ref, sp_ref,
    ins, outs,
):
    lev = lax.axis_index("lev")
    smalls = [
        pltpu.make_async_copy(src, dst, ins.at[i])
        for i, (src, dst) in enumerate(
            ((scale_hbm, scale_ref), (att_hbm, att_ref), (attp_hbm, attp_ref), (oc_hbm, oc_ref), (m_hbm, m_ref))
        )
    ]
    backs = [pltpu.make_async_copy(back_hbm.at[:, t], back_ref.at[:, t], ins.at[5 + t]) for t in range(4)]
    advs = [pltpu.make_async_copy(adv_hbm.at[t], adv_ref.at[t], ins.at[9 + t]) for t in range(4)]
    for copy in smalls:
        copy.start()
    for t in range(4):
        backs[t].start()
        advs[t].start()
    for copy in smalls:
        copy.wait()
    row, col = iota((128, 128), 0), iota((128, 128), 1)
    same = row // 64 == col // 64
    before = jnp.where(same & (row < col), 1.0, 0.0).astype(BF16)
    every = jnp.where(same & (lev == 1), 1.0, 0.0).astype(BF16)
    sums = jnp.concatenate([before] * 3 + [every] * 3, axis=0)
    for c in range(4):
        att = att_ref[c]
        terms = jnp.concatenate(pieces(att) + pieces(attp_ref[c]), axis=1)
        path = jnp.dot(terms, sums, preferred_element_type=F32)
        caught = jnp.exp(-path) * (1.0 - jnp.exp(-att))
        wet = jnp.concatenate([m_ref[2 * c], m_ref[2 * c + 1]], axis=1).astype(F32)
        lanes = slice(c * 128, c * 128 + 128)
        warm = oc_ref[0, :, lanes] + warming_amount * wet * caught
        for out, value in ((w_ref, warm), (s_ref, oc_ref[1, :, lanes]), (u_ref, oc_ref[2, :, lanes]), (v_ref, oc_ref[3, :, lanes])):
            out[2 * c] = value[:, 0:64]
            out[2 * c + 1] = value[:, 64:128]
    done = [
        pltpu.make_async_copy(src, dst, outs.at[i])
        for i, (src, dst) in enumerate(((w_ref, w_hbm), (s_ref, s_hbm), (u_ref, u_hbm), (v_ref, v_hbm)))
    ]
    for copy in done:
        copy.start()
    for t in range(4):
        backs[t].wait()
        advs[t].wait()
        for c in range(4):
            react = back_ref[c, t].astype(jnp.int32).astype(F32) * scale_ref[c]
            new = (adv_ref[t, c] + react_step * react.reshape(128, 128)).T
            sp_ref[t, pl.ds(2 * c, 64, stride=8), :] = new[0:64]
            sp_ref[t, pl.ds(2 * c + 1, 64, stride=8), :] = new[64:128]
        done.append(pltpu.make_async_copy(sp_ref.at[t], sp_hbm.at[t], outs.at[4 + t]))
        done[-1].start()
    for copy in done:
        copy.wait()


def shards(
    nz,
    nx,
    potential_warmth,
    saltiness_anomaly,
    zonal_speed,
    meridional_speed,
    marine_indicator,
    species_concentrations,
    coupling_matrix,
    species_guild_number,
    guild_extinction_coefficient,
):
    tiles = [
        jnp.transpose(a, (1, 2, 0))
        for a in (potential_warmth, saltiness_anomaly, zonal_speed, meridional_speed, marine_indicator)
    ]
    species = species_concentrations.reshape(4, 512, 128)
    dma = pltpu.SemaphoreType.DMA
    tile = pltpu.VMEM((8, 8, 64), F32)
    row, column = pltpu.VMEM((16, 64, 128), F32), pltpu.VMEM((16, 128), F32)
    tall, flat = pltpu.VMEM((16, 80, 128), F32), pltpu.VMEM((1280, 128), F32)
    edge = pltpu.VMEM((16, 8, 128), F32)
    adv, back, scale, att, attp, ocean = pl.pallas_call(
        functools.partial(step_kernel, nz, nx),
        out_shape=(
            sds((4, 4, 128, 128)),
            sds((4, 4, nz, 8, 128), I16),
            sds((4, nz, 1, 128)),
            sds((4, 8, 128)),
            sds((4, 8, 128)),
            sds((4, 8, 512)),
        ),
        in_specs=[pl.BlockSpec(memory_space=pltpu.HBM)] * 9,
        out_specs=(pl.BlockSpec(memory_space=pltpu.HBM),) * 6,
        scratch_shapes=[pltpu.VMEM((nz, 8, lanes), F32) for lanes in (SPEEDS, WATER, 512, 640, 512, 640)]
        + [pltpu.VMEM((4, 16, 80, 128), F32)]
        + [tile] * 4
        + [
            pltpu.VMEM((8, 8, 64), jnp.int32),
            pltpu.VMEM((4, 512, 128), F32),
            pltpu.VMEM((8, SPEEDS), F32),
            pltpu.VMEM((8, WATER), F32),
            pltpu.VMEM((8, 128), F32),
            pltpu.VMEM((8, 128), F32),
            dma((6,)),
            dma((2, 2, nz)),
        ]
        + [dma((2, nz))] * 5
        + [dma((6,))] * 2
        + [row] * 5
        + [edge, row, row, row, column, column]
        + [
            pltpu.VMEM((64, 64), BF16),
            pltpu.VMEM((1, 64), jnp.int32),
            pltpu.VMEM((1, 8), F32),
            dma((3,)),
            dma((14,)),
            pltpu.VMEM((4, 4, 128, 128), F32),
            pltpu.VMEM((4, 8, 128), F32),
            pltpu.VMEM((4, 8, 512), F32),
        ]
        + [tall, tall, flat, flat, tall, tall, flat, tall]
        + [
            pltpu.VMEM((128, 128), F32),
            flat,
            pltpu.VMEM((9, 128, 128), F32),
            pltpu.VMEM((9, 128, 128), F32),
            pltpu.VMEM((4, 128, 128), F32),
            pltpu.VMEM((4, 128, 128), F32),
            pltpu.VMEM((8, 64, 128), F32),
            edge,
            pltpu.VMEM((544, 512), BF16),
            pltpu.VMEM((4, nz, 8, 512), BF16),
            pltpu.VMEM((4, nz, 8, 512), BF16),
            pltpu.VMEM((4, 4, nz, 8, 128), I16),
            pltpu.VMEM((4, nz, 1, 128), F32),
        ]
        + [dma((4, nz))] * 4
        + [dma((2,))] * 2
        + [dma((4, nz))] * 2,
        compiler_params=pltpu.CompilerParams(collective_id=0, has_side_effects=True, vmem_limit_bytes=60 << 20),
        name="step",
    )(
        *tiles, species, coupling_matrix,
        species_guild_number.reshape(1, 64), guild_extinction_coefficient.reshape(1, 8),
    )

    hbm = pl.BlockSpec(memory_space=pltpu.HBM)
    warm, salt, zonal, merid, final = pl.pallas_call(
        final_kernel,
        out_shape=(sds((8, 8, 64)),) * 4 + (sds((4, 512, 128)),),
        in_specs=[hbm] * 7,
        out_specs=(hbm,) * 5,
        scratch_shapes=[
            pltpu.VMEM((4, 4, 128, 128), F32),
            pltpu.VMEM((4, 4, nz, 8, 128), I16),
            pltpu.VMEM((4, nz, 1, 128), F32),
            pltpu.VMEM((4, 8, 128), F32),
            pltpu.VMEM((4, 8, 128), F32),
            pltpu.VMEM((4, 8, 512), F32),
            pltpu.VMEM((8, 8, 64), jnp.int32),
        ]
        + [tile] * 4
        + [pltpu.VMEM((4, 512, 128), F32), dma((13,)), dma((8,))],
        compiler_params=pltpu.CompilerParams(vmem_limit_bytes=60 << 20),
        name="final",
    )(adv, back, scale, att, attp, ocean, tiles[4])
    warm, salt, zonal, merid = (jnp.transpose(a, (2, 0, 1)) for a in (warm, salt, zonal, merid))
    return warm, salt, zonal, merid, final.reshape(4, 64, 8, 128)


def solution(mesh):
    tile, tracers = P("lev", "cols", "trc"), P("trc", "lev", "cols", None)
    return jax.shard_map(
        functools.partial(shards, mesh.shape["trc"], mesh.shape["cols"]),
        mesh=mesh,
        in_specs=(tile, tile, tile, tile, tile, tracers, P(), P(), P()),
        out_specs=(tile, tile, tile, tile, tracers),
        check_vma=False,
    )
```

```python
import functools

import jax
import jax.numpy as jnp
from jax import lax
from jax.experimental import pallas as pl
from jax.experimental.pallas import tpu as pltpu
from jax.sharding import PartitionSpec as P

MESH = pl.DeviceIdType.MESH
F32 = jnp.float32
BF16 = jnp.bfloat16
I16 = jnp.int16

viscosity = 0.2
buoyancy = 0.25
marine_advance = 0.05
tracer_step = 0.2
level_step = 0.04
react_step = 0.25
warming_amount = 60.0

SPEEDS, DENSITY, WATER = 1024, 640, 1024


def sds(shape, dtype=F32):
    return jax.ShapeDtypeStruct(shape, dtype)


def iota(shape, axis):
    return lax.broadcasted_iota(jnp.int32, shape, axis)


def pieces(value):
    first = value.astype(BF16)
    rest = value - first.astype(F32)
    second = rest.astype(BF16)
    third = (rest - second.astype(F32)).astype(BF16)
    return first, second, third


def minmod_half(left, right):
    return jnp.maximum(jnp.minimum(left, right), jnp.minimum(jnp.maximum(left, right), 0.0))


def gather_kernel(
    nz, nx, t_hbm, s_hbm, u_hbm, v_hbm, m_hbm, sp_hbm,
    ga, gb, gt, la, lb, lt, ha, hb, ht, se,
    t_in, s_in, u_in, v_in, m_in, sp_in, a_own, b_own, t_own, d_own, d_peer,
    ins, zs, zr, ls, lr, hs, hr, ss, sr, ts, tr,
):
    z, x, lev = lax.axis_index("trc"), lax.axis_index("cols"), lax.axis_index("lev")
    zup, zdn = {"trc": (z + 1) % nz}, {"trc": (z + nz - 1) % nz}
    xup, xdn = {"cols": (x + 1) % nx}, {"cols": (x + nx - 1) % nx}
    peer = {"lev": 1 - lev}
    loads = [
        pltpu.make_async_copy(src, dst, ins.at[i])
        for i, (src, dst) in enumerate(
            ((u_hbm, u_in), (v_hbm, v_in), (t_hbm, t_in), (s_hbm, s_in), (m_hbm, m_in), (sp_hbm, sp_in))
        )
    ]
    for load in loads:
        load.start()
    for ref in (gt, lt, ht):
        ref[...] = jnp.zeros_like(ref)
    barrier = pltpu.get_barrier_semaphore()
    two_up, two_dn = {"trc": (z + 2) % nz}, {"trc": (z + nz - 2) % nz}
    for other in (zup, zdn, two_up, two_dn, xup, xdn, peer):
        pl.semaphore_signal(barrier, inc=1, device_id=other, device_id_type=MESH)

    def rdma(src, dst, send, recv, to):
        return pltpu.make_async_remote_copy(
            src_ref=src, dst_ref=dst, send_sem=send, recv_sem=recv, device_id=to, device_id_type=MESH
        )

    wholes, lefts, rights = (ga, gb), (la, lb), (ha, hb)
    upper, lower = (512, 256), (512, 384)

    def along(k, src, source, way, hop):
        to = {"trc": (z + (hop if way == 0 else nz - hop)) % nz}
        return rdma(src, wholes[k].at[source], zs.at[k], zr.at[k, source], to)

    def to_right(k, src, source):
        return rdma(src.at[:, upper[k] :], lefts[k].at[source], ls.at[k], lr.at[k], xup)

    def to_left(k, src, source):
        return rdma(src.at[:, : lower[k]], rights[k].at[source], hs.at[k], hr.at[k], xdn)

    def fill(block, refs, high):
        for f, ref in enumerate(refs):
            for k in range(4):
                off = (0 if k < 2 else high) + f * 256 + (k % 2) * 128
                block[:, off : off + 128] = jnp.concatenate([ref[2 * k], ref[2 * k + 1]], axis=1)

    def begin(k, block):
        for hop in (2, 1):
            along(k, block, z, 0, hop).start()
            along(k, block, z, 1, hop).start()
        to_right(k, block, z).start()
        to_left(k, block, z).start()
        wholes[k][z] = block[...]

    loads[0].wait()
    loads[1].wait()
    fill(a_own, (u_in, v_in), 512)
    pl.semaphore_wait(barrier, 7)
    begin(0, a_own)

    for load in loads[2:5]:
        load.wait()
    rho = u_in
    lane = iota((8, 128), 1)
    counts = jnp.zeros((8, 128), F32)
    dense = jnp.zeros((8, 128), F32)
    for i in range(8):
        counts = counts + jnp.where(lane == i, jnp.sum(m_in[i].astype(F32), axis=1, keepdims=True), 0.0)
        rho[i] = 0.8 * s_in[i] - 0.2 * t_in[i]
        column = jnp.sum(rho[i], axis=1, keepdims=True)
        dense = dense + jnp.where(lane == i + 8, column, 0.0)
    d_own[...] = dense
    above = rdma(d_own, d_peer, ss.at[5], sr.at[5], peer)
    above.start()
    fill(b_own, (rho,), 384)
    fill(t_own, (t_in, s_in), 512)

    loads[5].wait()

    def spread(t, carry):
        for i in range(8):
            se[t, 4 + i, 8:72, :] = sp_in[t, pl.ds(i, 64, stride=8), :]
        return carry

    lax.fori_loop(0, 4, spread, 0)
    near = pl.multiple_of((1 - lev) * 56 + 8, 8)
    there = pl.multiple_of(lev * 72, 8)
    own_x = rdma(se.at[:, 8:12, 8:72], se.at[:, 0:4, 8:72], ss.at[0], sr.at[0], xup)
    own_y = rdma(se.at[:, 4:8, 8:72], se.at[:, 12:16, 8:72], ss.at[1], sr.at[1], xdn)
    parts = [
        rdma(se.at[:, low:high, pl.ds(near, 8)], se.at[:, low:high, pl.ds(there, 8)], ss.at[i], sr.at[i], peer)
        for i, low, high in ((2, 4, 12), (3, 0, 4), (4, 12, 16))
    ]
    above.wait_recv()
    b_own[:, 256:384] = counts + jnp.where(lev == 1, d_peer[...], 0.0)
    begin(1, b_own)
    near_water = [
        rdma(t_own, gt.at[z], ts.at[0], tr.at[0], zup),
        rdma(t_own, gt.at[z], ts.at[1], tr.at[1], zdn),
        rdma(t_own.at[:, 512:], lt.at[z], ts.at[2], tr.at[2], xup),
        rdma(t_own.at[:, :512], ht.at[z], ts.at[3], tr.at[3], xdn),
    ]
    for copy in near_water:
        copy.start()
    gt[z] = t_own[...]
    own_x.start()
    own_y.start()
    parts[0].start()

    def clear(t, carry):
        se[t, :, pl.ds(there, 8), :] = jnp.zeros((16, 8, 128), F32)
        return carry

    lax.fori_loop(0, 4, clear, 0)
    half = nz // 2
    for step in range(1, half + 1):
        came = []
        for k in range(2):
            for way, source in ((0, (z + nz - step) % nz), (1, (z + step) % nz))[: 2 if step < half else 1]:
                block = wholes[k].at[source]
                along(k, block, source, way, 1).wait_recv()
                if step % 2 == 0:
                    for hop in (2, 1):
                        if step + hop <= half - way:
                            along(k, block, source, way, hop).start()
                came.append((k, block, source))
        for k, block, source in came:
            to_right(k, block, source).start()
            to_left(k, block, source).start()
        if step == 3:
            own_x.wait_recv()
            parts[1].start()
            own_y.wait_recv()
            parts[2].start()

    for part in parts:
        part.wait_recv()
        part.wait_send()

    for k in range(2):
        for ref, send, recv in ((lefts[k], ls, lr), (rights[k], hs, hr)):
            copies = rdma(ref, ref, send.at[k], recv.at[k], xup)
            copies.wait_recv()
            copies.wait_send()
        blocks = wholes[k].at[0 : nz - 1]
        rdma(blocks, blocks, zs.at[k], zr.at[k, z], zup).wait_send()
    for copy in near_water:
        copy.wait_recv()
        copy.wait_send()
    for copy in (own_x, own_y, above):
        copy.wait_send()


def flow_kernel(ga, gb, gt, la, lb, lt, ha, hb, ht, uf_ref, vf_ref, fv_ref, t_ref, s_ref, bnd_ref, uu, vv, rho, pp, cnt, top):
    lev = lax.axis_index("lev")
    sides = (
        ((uu, vv), ((la, 0), (ga, 0), (ga, 512), (ha, 0))),
        ((t_ref, s_ref), ((lt, 0), (gt, 0), (gt, 512), (ht, 0))),
        ((rho,), ((lb, 128), (gb, 0), (gb, 384), (hb, 0))),
    )
    for fields, sources in sides:
        for part, (ref, base) in enumerate(sources):
            for f, out in enumerate(fields):
                for k in range(2):
                    off = base + f * 256 + k * 128
                    r = part * 4 + k * 2
                    out[r : r + 2] = ref[:, :, off : off + 128].reshape(128, 128).T.reshape(2, 64, 128)
    aux = gb[:, :, 256:384].reshape(128, 128).T
    aux_l = lb[:, :, 0:128].reshape(128, 128).T
    aux_h = hb[:, :, 256:384].reshape(128, 128).T
    cnt[0:4], cnt[4:12], cnt[12:16] = aux_l[4:8], aux[0:8], aux_h[0:4]
    top[0:4], top[4:12], top[12:16] = aux_l[12:16], aux[8:16], aux_h[8:12]

    row, col = iota((64, 64), 0), iota((64, 64), 1)
    down = jnp.where(col < row, 1.0, jnp.where(col == row, 0.5, 0.0)).astype(BF16)
    down = jnp.concatenate([down] * 3, axis=1)
    deep = jnp.where(col >= row, 1.0, 0.0).astype(BF16)
    deep = jnp.concatenate([deep] * 3, axis=1)
    for r in range(16):
        total = jnp.dot(down, jnp.concatenate(pieces(rho[r]), axis=0), preferred_element_type=F32)
        pp[r] = buoyancy * (top[r : r + 1] + total)

    level = iota((64, 128), 0).astype(F32)
    uf_ref[0] = jnp.zeros((64, 128), F32)
    vf_ref[0] = jnp.zeros((64, 128), F32)
    for r in (14, 15):
        uf_ref[r] = jnp.zeros((64, 128), F32)
        vf_ref[r] = jnp.zeros((64, 128), F32)
    for r in range(1, 14):
        here, east = cnt[r : r + 1], cnt[r + 1 : r + 2]
        north = pltpu.roll(jnp.broadcast_to(here, (8, 128)), 127, 1)[0:1]
        p, u, v = pp[r], uu[r], vv[r]
        lap_u = uu[r + 1] + uu[r - 1] + pltpu.roll(u, 127, 1) + pltpu.roll(u, 1, 1) - 4.0 * u
        lap_v = vv[r + 1] + vv[r - 1] + pltpu.roll(v, 127, 1) + pltpu.roll(v, 1, 1) - 4.0 * v
        new_u = u + marine_advance * (p - pp[r + 1] + viscosity * lap_u)
        new_v = v + marine_advance * (p - pltpu.roll(p, 127, 1) + viscosity * lap_v)
        uf_ref[r] = jnp.where(level < jnp.minimum(here, east), new_u, 0.0)
        vf_ref[r] = jnp.where(level < jnp.minimum(here, north), new_v, 0.0)

    zero = jnp.zeros((1, 128), F32)
    first = lev == 0
    for r in range(16):
        if 2 <= r < 14:
            u, v = uf_ref[r], vf_ref[r]
            div = u - uf_ref[r - 1] + v - pltpu.roll(v, 1, 1)
            fv = jnp.dot(deep, jnp.concatenate(pieces(div), axis=0), preferred_element_type=F32)
            fv_ref[r] = fv
            flow = fv[0:1]
        else:
            fv_ref[r] = jnp.zeros((64, 128), F32)
            flow = zero
        u2 = jnp.where(first, uf_ref[r, 62:64], uf_ref[r, 0:2])
        v2 = jnp.where(first, vf_ref[r, 62:64], vf_ref[r, 0:2])
        t1 = jnp.where(first, t_ref[r, 63:64], t_ref[r, 0:1])
        s1 = jnp.where(first, s_ref[r, 63:64], s_ref[r, 0:1])
        bnd_ref[r] = jnp.concatenate([u2, v2, flow, t1, s1, zero], axis=0)


def fill_matrix(c_ref, guild_ref, light_ref, w_ref):
    kinds = iota((8, 64), 0) == guild_ref[...]
    light = jnp.sum(jnp.where(iota((8, 8), 0) == iota((8, 8), 1), light_ref[...], 0.0), axis=1, keepdims=True)
    absorb = jnp.sum(jnp.where(kinds, light, 0.0), axis=0, keepdims=True)
    absorb = jnp.broadcast_to(absorb, (8, 64))
    place, across = iota((512, 64), 0), iota((64, 512), 1)
    spread = jnp.where(place // 8 % 16 * 4 + place // 128 == iota((512, 64), 1), 1.0, 0.0).astype(BF16)
    across = jnp.where(across // 8 % 16 * 4 + across // 128 == iota((64, 512), 0), 1.0, 0.0).astype(BF16)
    tall = jnp.dot(spread, c_ref[...], preferred_element_type=F32).astype(BF16)
    wide = jnp.dot(tall, across, preferred_element_type=F32)
    w_ref[0:512] = jnp.where(iota((512, 512), 0) % 8 == iota((512, 512), 1) % 8, wide, 0.0).astype(BF16)
    own = iota((8, 512), 0) == iota((8, 512), 1) % 8
    rows = []
    for part in pieces(absorb):
        line = jnp.dot(part, across, preferred_element_type=F32)
        rows.append(jnp.where(own, line, 0.0))
    rows.append(jnp.zeros((8, 512), F32))
    w_ref[512:544] = jnp.concatenate(rows, axis=0).astype(BF16)


def react_kernel(
    nz, uf_ref, vf_ref, fv_ref, t_ref, s_ref, edge_ref, se_ref, c_ref, guild_ref, light_ref,
    adv_ref, back_ref, scale_ref, att_ref, attp_ref, oc_ref, adv_out, att_out, oc_out, out_sems,
    up, um, vp, vm, fp, fm, q1, ex, tr, yd, vpt, vmt, vpu, vmu, rest, bnd_ref, w_ref, send_ref, got, res, sizes,
    s1, r1, s2, r2, s3, r3, s4, r4, s5, r5,
):
    z, lev = lax.axis_index("trc"), lax.axis_index("lev")
    first = lev == 0
    sub = iota((8, 128), 0)
    peer = {"lev": 1 - lev}
    def rdma(src, dst, send, recv, to):
        return pltpu.make_async_remote_copy(
            src_ref=src, dst_ref=dst, send_sem=send, recv_sem=recv, device_id=to, device_id_type=MESH
        )

    def each(body):
        def one(i, carry):
            d = nz // 2 + (i + 1) // 2 * (1 - i % 2 * 2)
            body((z + d) % nz)
            return carry

        lax.fori_loop(0, nz - 1, one, 0)

    others = pl.ds(0, nz - 1)

    def to_device(to):
        return peer if to is others else {"trc": to}

    def out(t, to, at):
        return rdma(send_ref.at[t, to], got.at[t, at], s1.at[t], r1.at[t], to_device(to))

    def last(c, to, at):
        lanes = slice(c * 128, c * 128 + 128)
        return rdma(send_ref.at[3, to, :, lanes], got.at[3, at, :, lanes], s5.at[c], r5.at[c], to_device(to))

    def home(c, to, at):
        return rdma(res.at[c, :, to], back_ref.at[c, :, at], s2.at[c], r2.at[c], to_device(to))

    def size(c, to, at):
        return rdma(sizes.at[c, to], scale_ref.at[c, at], s4.at[c], r4.at[c], to_device(to))


    def stored(t):
        return pltpu.make_async_copy(adv_ref.at[t], adv_out.at[t], out_sems.at[t])

    def own_back(c):
        return pltpu.make_async_copy(res.at[c, :, z], back_ref.at[c, :, z], out_sems.at[4 + c])

    def own_scale(c):
        return pltpu.make_async_copy(sizes.at[c, z], scale_ref.at[c, z], out_sems.at[8 + c])

    ocean = pltpu.make_async_copy(oc_ref, oc_out, out_sems.at[12])
    shades = pltpu.make_async_copy(att_ref, att_out, out_sems.at[13])
    edges = rdma(edge_ref.at[1:14], bnd_ref.at[1:14], s3.at[0], r3.at[0], peer)
    edges.start()
    mine = pl.multiple_of(z * 8, 8)
    for f, ref in enumerate((uf_ref, vf_ref)):
        for k in range(4):
            tr[...] = ref[4 + 2 * k : 6 + 2 * k].reshape(128, 128).T
            oc_ref[2 + f, :, k * 128 : k * 128 + 128] = tr[pl.ds(mine, 8), :]
    fill_matrix(c_ref, guild_ref, light_ref, w_ref)
    bnd_ref[0] = jnp.zeros((8, 128), F32)
    edges.wait_recv()

    def rows(r):
        return pl.ds(pl.multiple_of(r * 80, 8), 80)

    def around(own, above, below):
        return jnp.concatenate(
            [jnp.where(first, 0.0, above), own, jnp.where(first, below, 0.0)], axis=0
        )

    def faces(r, carry):
        edge = bnd_ref[r]
        edge_w = bnd_ref[r - 1]
        pos = pltpu.roll(edge, 6, 0)
        u_ext = around(uf_ref[r], jnp.where(sub >= 6, pos, 0.0), jnp.where(sub < 2, edge, 0.0))
        two = pltpu.roll(edge, 4, 0)
        low = pltpu.roll(edge, 6, 0)
        v_ext = around(vf_ref[r], jnp.where(sub >= 6, two, 0.0), jnp.where(sub < 2, low, 0.0))
        d2 = edge[0:2] - edge_w[0:2] + edge[2:4] - pltpu.roll(edge, 1, 1)[2:4]
        d0, d1 = d2[0:1], d2[1:2]
        flow = jnp.where(first, edge[4:5], 0.0)
        f_own = fv_ref[r] + flow
        above = jnp.where(sub == 7, f_own[0:1] + d1, jnp.where(sub == 6, f_own[0:1] + d1 + d0, 0.0))
        below = jnp.where(
            sub == 0, flow, jnp.where(sub == 1, flow - d0, jnp.where(sub == 2, flow - d0 - d1, 0.0))
        )
        surface = jnp.where((iota((64, 128), 0) == 0) & first, 0.0, f_own)
        f_ext = level_step * around(surface, above, below)
        u_ext = tracer_step * u_ext
        v_ext = tracer_step * v_ext
        up[r], um[r] = jnp.maximum(u_ext, 0.0), jnp.minimum(u_ext, 0.0)
        vp[rows(r)], vm[rows(r)] = jnp.maximum(v_ext, 0.0), jnp.minimum(v_ext, 0.0)
        fp[r], fm[r] = jnp.maximum(f_ext, 0.0), jnp.minimum(f_ext, 0.0)
        return carry

    lax.fori_loop(1, 14, faces, 0)

    def turn_faces(ref, wide, narrow):
        for c in range(9):
            wide[c] = ref[64 + 128 * c : 192 + 128 * c].T
        for k in range(4):
            row = (4 + 2 * k) * 80 + 8
            both = jnp.concatenate([ref[row : row + 64], ref[row + 80 : row + 144]], axis=0)
            narrow[k] = both.T

    turn_faces(vp, vpt, vpu)
    turn_faces(vm, vmt, vmu)

    def along_y(q, plus, minus):
        north = 0.5 * (pltpu.roll(q, 127, 0) - q)
        slope = minmod_half(pltpu.roll(north, 1, 0), north)
        flux = plus * (q + slope) + minus * pltpu.roll(q - slope, 127, 0)
        return flux - pltpu.roll(flux, 1, 0)

    def sweep(load, store, start, stop):
        d_a = 0.5 * (load(start - 1) - load(start - 2))
        d_b = 0.5 * (load(start) - load(start - 1))
        d_c = 0.5 * (load(start + 1) - load(start))
        right = load(start - 1) + minmod_half(d_a, d_b)
        slope = minmod_half(d_b, d_c)
        flux = up[start - 1] * right + um[start - 1] * (load(start) - slope)

        def one(r, carry):
            d_here, right, flux = carry
            q, q_e = load(r), load(r + 1)
            d_next = 0.5 * (load(r + 2) - q_e)
            slope = minmod_half(d_here, d_next)
            flux_e = up[r] * right + um[r] * (q_e - slope)
            change = flux_e - flux
            right_e = q_e + slope
            below = 0.5 * (pltpu.roll(q, 79, 0) - q)
            slope = minmod_half(pltpu.roll(below, 1, 0), below)
            flux_v = fp[r] * pltpu.roll(q + slope, 1, 0) + fm[r] * (q - slope)
            change = change + (pltpu.roll(flux_v, 79, 0) - flux_v)
            store(r, q - change)
            return d_next, right_e, flux_e

        lax.fori_loop(start, stop, one, (d_c, load(start) + slope, flux))

    def tracer(t, carry):
        def first_load(r):
            return se_ref[t, r]

        def first_store(r, value):
            q1[rows(r)] = value - yd[rows(r)]

        def second_load(r):
            return q1[rows(r)]

        def second_store(r, value):
            rest[r - 4] = value[8:72]

        for c in range(9):
            start, stop = 64 + 128 * c, 192 + 128 * c
            q = [se_ref[t, r, max(start - r * 80, 0) : min(stop - r * 80, 80)] for r in range(start // 80, (stop + 79) // 80)]
            q = jnp.concatenate(q, axis=0).T
            yd[64 + 128 * c : 192 + 128 * c] = along_y(q, vpt[c], vmt[c]).T
        sweep(first_load, first_store, 2, 14)
        sweep(second_load, second_store, 4, 12)
        for k in range(4):
            row = (4 + 2 * k) * 80 + 8
            q = jnp.concatenate([q1[row : row + 64], q1[row + 80 : row + 144]], axis=0).T
            new = rest[2 * k : 2 * k + 2].reshape(128, 128).T - along_y(q, vpu[k], vmu[k])
            adv_ref[t, k] = new
            send_ref[t, :, :, k * 128 : k * 128 + 128] = new.reshape(16, 8, 128).astype(BF16)

        @pl.when(t < 3)
        def _():
            each(lambda to: out(t, to, z).start())

        got[t, z] = send_ref[t, z]
        stored(t).start()
        return carry

    lax.fori_loop(0, 4, tracer, 0)
    for c in range(4):
        each(lambda to: last(c, to, z).start())

    for f, ref in enumerate((t_ref, s_ref)):
        for r in range(3, 13):
            edge = bnd_ref[r][5 + f : 6 + f]
            ex[r] = around(ref[r], jnp.where(sub == 7, edge, 0.0), jnp.where(sub == 0, edge, 0.0))

        def donor(r, flux_w):
            c = ex[r]
            flux = up[r] * c + um[r] * ex[r + 1]
            flux_n = vp[rows(r)] * c + vm[rows(r)] * pltpu.roll(c, 127, 1)
            flux_v = fp[r] * pltpu.roll(c, 1, 0) + fm[r] * c
            wide = flux - flux_w + (flux_n - pltpu.roll(flux_n, 1, 1))
            tall = pltpu.roll(flux_v, 79, 0) - flux_v
            new = c - (marine_advance / tracer_step) * wide - (marine_advance / level_step) * tall
            q1[rows(r)] = new
            return flux

        lax.fori_loop(4, 12, donor, up[3] * ex[3] + um[3] * ex[4])
        for k in range(4):
            row = (4 + 2 * k) * 80 + 8
            both = jnp.concatenate([q1[row : row + 64], q1[row + 80 : row + 144]], axis=0)
            tr[...] = both.T
            oc_ref[f, :, k * 128 : k * 128 + 128] = tr[pl.ds(mine, 8), :]
    ocean.start()

    for t in range(3):
        out(t, others, others).wait_recv()
    for c in range(4):
        last(c, others, others).wait_recv()
        values = got[:, :, :, c * 128 : c * 128 + 128].reshape(512, 128)
        values = jnp.dot(w_ref[...], values, preferred_element_type=F32)
        att_ref[c] = values[512:520] + values[520:528] + values[528:536]
        values = values[0:512].reshape(4, nz, 8, 128)
        largest = jnp.max(jnp.max(jnp.abs(values), axis=0), axis=1, keepdims=True)
        largest = jnp.maximum(largest, 1e-30)
        sizes[c] = largest * (1.0 / 32767.0)
        coded = jnp.round(values * (32767.0 / largest)[None])
        res[c] = coded.astype(jnp.int32).astype(I16)
        each(lambda to: (home(c, to, z).start(), size(c, to, z).start()))
        own_back(c).start()
        own_scale(c).start()
    shade = rdma(att_ref, attp_ref, s3.at[1], r3.at[1], peer)
    shade.start()
    shades.start()
    for c in range(4):
        home(c, others, others).wait_recv()
        size(c, others, others).wait_recv()
        last(c, others, others).wait_send()
        if c < 3:
            out(c, others, others).wait_send()
        home(c, others, others).wait_send()
        size(c, others, others).wait_send()
    shade.wait_recv()
    shade.wait_send()
    edges.wait_send()
    for c in range(4):
        stored(c).wait()
        own_back(c).wait()
        own_scale(c).wait()
    ocean.wait()
    shades.wait()


GATHERED = 10
LOADED = 11
ARRIVALS = 11
FLOWS = 6


def step_kernel(nz, nx, *refs):
    fields, params, outs, scratch = refs[:6], refs[6:9], refs[9:15], refs[15:]
    gathered, scratch = scratch[:GATHERED], scratch[GATHERED:]
    loaded, scratch = scratch[: LOADED + ARRIVALS], scratch[LOADED + ARRIVALS :]
    flows, scratch = scratch[:FLOWS], scratch[FLOWS:]
    temporary, scratch = scratch[:6], scratch[6:]
    held, scratch = scratch[:3], scratch[3:]
    param_sems, out_sems, adv_ref, att_ref, oc_ref = scratch[:5]
    loads = [pltpu.make_async_copy(src, dst, param_sems.at[i]) for i, (src, dst) in enumerate(zip(params, held))]
    for load in loads:
        load.start()
    gather_kernel(nz, nx, *fields, *gathered, *loaded)
    flow_kernel(*gathered[:9], *flows, *temporary)
    for load in loads:
        load.wait()
    adv_out, back_ref, scale_ref, att_out, attp_ref, oc_out = outs
    react_kernel(
        nz, *flows, gathered[9], *held, adv_ref, back_ref, scale_ref, att_ref, attp_ref, oc_ref,
        adv_out, att_out, oc_out, out_sems, *scratch[5:]
    )


def final_kernel(
    adv_hbm, back_hbm, scale_hbm, att_hbm, attp_hbm, oc_hbm, m_hbm,
    w_hbm, s_hbm, u_hbm, v_hbm, sp_hbm,
    adv_ref, back_ref, scale_ref, att_ref, attp_ref, oc_ref, m_ref, w_ref, s_ref, u_ref, v_ref, sp_ref,
    ins, outs,
):
    lev = lax.axis_index("lev")
    smalls = [
        pltpu.make_async_copy(src, dst, ins.at[i])
        for i, (src, dst) in enumerate(
            ((scale_hbm, scale_ref), (att_hbm, att_ref), (attp_hbm, attp_ref), (oc_hbm, oc_ref), (m_hbm, m_ref))
        )
    ]
    backs = [pltpu.make_async_copy(back_hbm.at[:, t], back_ref.at[:, t], ins.at[5 + t]) for t in range(4)]
    advs = [pltpu.make_async_copy(adv_hbm.at[t], adv_ref.at[t], ins.at[9 + t]) for t in range(4)]
    for copy in smalls:
        copy.start()
    for t in range(4):
        backs[t].start()
        advs[t].start()
    for copy in smalls:
        copy.wait()
    row, col = iota((128, 128), 0), iota((128, 128), 1)
    same = row // 64 == col // 64
    before = jnp.where(same & (row < col), 1.0, 0.0).astype(BF16)
    every = jnp.where(same & (lev == 1), 1.0, 0.0).astype(BF16)
    sums = jnp.concatenate([before] * 3 + [every] * 3, axis=0)
    for c in range(4):
        att = att_ref[c]
        terms = jnp.concatenate(pieces(att) + pieces(attp_ref[c]), axis=1)
        path = jnp.dot(terms, sums, preferred_element_type=F32)
        caught = jnp.exp(-path) * (1.0 - jnp.exp(-att))
        wet = jnp.concatenate([m_ref[2 * c], m_ref[2 * c + 1]], axis=1).astype(F32)
        lanes = slice(c * 128, c * 128 + 128)
        warm = oc_ref[0, :, lanes] + warming_amount * wet * caught
        for out, value in ((w_ref, warm), (s_ref, oc_ref[1, :, lanes]), (u_ref, oc_ref[2, :, lanes]), (v_ref, oc_ref[3, :, lanes])):
            out[2 * c] = value[:, 0:64]
            out[2 * c + 1] = value[:, 64:128]
    done = [
        pltpu.make_async_copy(src, dst, outs.at[i])
        for i, (src, dst) in enumerate(((w_ref, w_hbm), (s_ref, s_hbm), (u_ref, u_hbm), (v_ref, v_hbm)))
    ]
    for copy in done:
        copy.start()
    for t in range(4):
        backs[t].wait()
        advs[t].wait()
        for c in range(4):
            react = back_ref[c, t].astype(jnp.int32).astype(F32) * scale_ref[c]
            new = (adv_ref[t, c] + react_step * react.reshape(128, 128)).T
            sp_ref[t, pl.ds(2 * c, 64, stride=8), :] = new[0:64]
            sp_ref[t, pl.ds(2 * c + 1, 64, stride=8), :] = new[64:128]
        done.append(pltpu.make_async_copy(sp_ref.at[t], sp_hbm.at[t], outs.at[4 + t]))
        done[-1].start()
    for copy in done:
        copy.wait()


def shards(
    nz,
    nx,
    potential_warmth,
    saltiness_anomaly,
    zonal_speed,
    meridional_speed,
    marine_indicator,
    species_concentrations,
    coupling_matrix,
    species_guild_number,
    guild_extinction_coefficient,
):
    tiles = [
        jnp.transpose(a, (1, 2, 0))
        for a in (potential_warmth, saltiness_anomaly, zonal_speed, meridional_speed, marine_indicator)
    ]
    species = species_concentrations.reshape(4, 512, 128)
    dma = pltpu.SemaphoreType.DMA
    tile = pltpu.VMEM((8, 8, 64), F32)
    row, column = pltpu.VMEM((16, 64, 128), F32), pltpu.VMEM((16, 128), F32)
    tall, flat = pltpu.VMEM((16, 80, 128), F32), pltpu.VMEM((1280, 128), F32)
    edge = pltpu.VMEM((16, 8, 128), F32)
    adv, back, scale, att, attp, ocean = pl.pallas_call(
        functools.partial(step_kernel, nz, nx),
        out_shape=(
            sds((4, 4, 128, 128)),
            sds((4, 4, nz, 8, 128), I16),
            sds((4, nz, 1, 128)),
            sds((4, 8, 128)),
            sds((4, 8, 128)),
            sds((4, 8, 512)),
        ),
        in_specs=[pl.BlockSpec(memory_space=pltpu.HBM)] * 9,
        out_specs=(pl.BlockSpec(memory_space=pltpu.HBM),) * 6,
        scratch_shapes=[pltpu.VMEM((nz, 8, lanes), F32) for lanes in (SPEEDS, DENSITY, WATER, 512, 384, 512, 512, 384, 512)]
        + [pltpu.VMEM((4, 16, 80, 128), F32)]
        + [tile] * 4
        + [
            pltpu.VMEM((8, 8, 64), jnp.int32),
            pltpu.VMEM((4, 512, 128), F32),
            pltpu.VMEM((8, SPEEDS), F32),
            pltpu.VMEM((8, DENSITY), F32),
            pltpu.VMEM((8, WATER), F32),
            pltpu.VMEM((8, 128), F32),
            pltpu.VMEM((8, 128), F32),
            dma((6,)),
            dma((2,)),
            dma((2, nz)),
        ]
        + [dma((2,))] * 4
        + [dma((6,))] * 2
        + [dma((4,))] * 2
        + [row] * 5
        + [edge, row, row, row, row, column, column]
        + [
            pltpu.VMEM((64, 64), BF16),
            pltpu.VMEM((1, 64), jnp.int32),
            pltpu.VMEM((1, 8), F32),
            dma((3,)),
            dma((14,)),
            pltpu.VMEM((4, 4, 128, 128), F32),
            pltpu.VMEM((4, 8, 128), F32),
            pltpu.VMEM((4, 8, 512), F32),
        ]
        + [tall, tall, flat, flat, tall, tall, flat, tall]
        + [
            pltpu.VMEM((128, 128), F32),
            flat,
            pltpu.VMEM((9, 128, 128), F32),
            pltpu.VMEM((9, 128, 128), F32),
            pltpu.VMEM((4, 128, 128), F32),
            pltpu.VMEM((4, 128, 128), F32),
            pltpu.VMEM((8, 64, 128), F32),
            edge,
            pltpu.VMEM((544, 512), BF16),
            pltpu.VMEM((4, nz, 8, 512), BF16),
            pltpu.VMEM((4, nz, 8, 512), BF16),
            pltpu.VMEM((4, 4, nz, 8, 128), I16),
            pltpu.VMEM((4, nz, 1, 128), F32),
        ]
        + [dma((4,))] * 4
        + [dma((2,))] * 2
        + [dma((4,))] * 4,
        compiler_params=pltpu.CompilerParams(collective_id=0, has_side_effects=True, vmem_limit_bytes=60 << 20),
        name="step",
    )(
        *tiles, species, coupling_matrix,
        species_guild_number.reshape(1, 64), guild_extinction_coefficient.reshape(1, 8),
    )

    hbm = pl.BlockSpec(memory_space=pltpu.HBM)
    warm, salt, zonal, merid, final = pl.pallas_call(
        final_kernel,
        out_shape=(sds((8, 8, 64)),) * 4 + (sds((4, 512, 128)),),
        in_specs=[hbm] * 7,
        out_specs=(hbm,) * 5,
        scratch_shapes=[
            pltpu.VMEM((4, 4, 128, 128), F32),
            pltpu.VMEM((4, 4, nz, 8, 128), I16),
            pltpu.VMEM((4, nz, 1, 128), F32),
            pltpu.VMEM((4, 8, 128), F32),
            pltpu.VMEM((4, 8, 128), F32),
            pltpu.VMEM((4, 8, 512), F32),
            pltpu.VMEM((8, 8, 64), jnp.int32),
        ]
        + [tile] * 4
        + [pltpu.VMEM((4, 512, 128), F32), dma((13,)), dma((8,))],
        compiler_params=pltpu.CompilerParams(vmem_limit_bytes=60 << 20),
        name="final",
    )(adv, back, scale, att, attp, ocean, tiles[4])
    warm, salt, zonal, merid = (jnp.transpose(a, (2, 0, 1)) for a in (warm, salt, zonal, merid))
    return warm, salt, zonal, merid, final.reshape(4, 64, 8, 128)


def solution(mesh):
    tile, tracers = P("lev", "cols", "trc"), P("trc", "lev", "cols", None)
    return jax.shard_map(
        functools.partial(shards, mesh.shape["trc"], mesh.shape["cols"]),
        mesh=mesh,
        in_specs=(tile, tile, tile, tile, tile, tracers, P(), P(), P()),
        out_specs=(tile, tile, tile, tile, tracers),
        check_vma=False,
    )
```

```python
import functools

import jax
import jax.numpy as jnp
from jax import lax
from jax.experimental import pallas as pl
from jax.experimental.pallas import tpu as pltpu
from jax.sharding import PartitionSpec as P

MESH = pl.DeviceIdType.MESH
F32 = jnp.float32
BF16 = jnp.bfloat16
I16 = jnp.int16

viscosity = 0.2
buoyancy = 0.25
marine_advance = 0.05
tracer_step = 0.2
level_step = 0.04
react_step = 0.25
warming_amount = 60.0

SPEEDS, DENSITY, WATER = 1024, 640, 1024


def sds(shape, dtype=F32):
    return jax.ShapeDtypeStruct(shape, dtype)


def iota(shape, axis):
    return lax.broadcasted_iota(jnp.int32, shape, axis)


def pieces(value):
    first = value.astype(BF16)
    rest = value - first.astype(F32)
    second = rest.astype(BF16)
    third = (rest - second.astype(F32)).astype(BF16)
    return first, second, third


def minmod_half(left, right):
    return jnp.maximum(jnp.minimum(left, right), jnp.minimum(jnp.maximum(left, right), 0.0))


def gather_kernel(
    nz, nx, t_hbm, s_hbm, u_hbm, v_hbm, m_hbm, sp_hbm,
    ga, gb, gt, la, lb, lt, ha, hb, ht, se,
    t_in, s_in, u_in, v_in, m_in, sp_in, a_own, b_own, t_own, d_own, d_peer,
    ins, zs, zr, ls, lr, hs, hr, ss, sr, ts, tr,
):
    z, x, lev = lax.axis_index("trc"), lax.axis_index("cols"), lax.axis_index("lev")
    zup, zdn = {"trc": (z + 1) % nz}, {"trc": (z + nz - 1) % nz}
    xup, xdn = {"cols": (x + 1) % nx}, {"cols": (x + nx - 1) % nx}
    peer = {"lev": 1 - lev}
    loads = [
        pltpu.make_async_copy(src, dst, ins.at[i])
        for i, (src, dst) in enumerate(
            ((u_hbm, u_in), (v_hbm, v_in), (t_hbm, t_in), (s_hbm, s_in), (m_hbm, m_in), (sp_hbm, sp_in))
        )
    ]
    for load in loads:
        load.start()
    for ref in (gt, lt, ht):
        ref[...] = jnp.zeros_like(ref)
    barrier = pltpu.get_barrier_semaphore()
    two_up, two_dn = {"trc": (z + 2) % nz}, {"trc": (z + nz - 2) % nz}
    for other in (zup, zdn, two_up, two_dn, xup, xdn, peer):
        pl.semaphore_signal(barrier, inc=1, device_id=other, device_id_type=MESH)

    def rdma(src, dst, send, recv, to):
        return pltpu.make_async_remote_copy(
            src_ref=src, dst_ref=dst, send_sem=send, recv_sem=recv, device_id=to, device_id_type=MESH
        )

    wholes, lefts, rights = (ga, gb), (la, lb), (ha, hb)
    upper, lower = (512, 256), (512, 384)

    def along(k, src, source, way, hop):
        to = {"trc": (z + (hop if way == 0 else nz - hop)) % nz}
        return rdma(src, wholes[k].at[source], zs.at[k], zr.at[k, source], to)

    def to_right(k, src, source):
        return rdma(src.at[:, upper[k] :], lefts[k].at[source], ls.at[k], lr.at[k], xup)

    def to_left(k, src, source):
        return rdma(src.at[:, : lower[k]], rights[k].at[source], hs.at[k], hr.at[k], xdn)

    def fill(block, refs, high):
        for f, ref in enumerate(refs):
            for k in range(4):
                off = (0 if k < 2 else high) + f * 256 + (k % 2) * 128
                block[:, off : off + 128] = jnp.concatenate([ref[2 * k], ref[2 * k + 1]], axis=1)

    def begin(k, block):
        for hop in (2, 1):
            along(k, block, z, 0, hop).start()
            along(k, block, z, 1, hop).start()
        to_right(k, block, z).start()
        to_left(k, block, z).start()
        wholes[k][z] = block[...]

    loads[0].wait()
    loads[1].wait()
    fill(a_own, (u_in, v_in), 512)
    pl.semaphore_wait(barrier, 7)
    begin(0, a_own)

    for load in loads[2:5]:
        load.wait()
    rho = u_in
    lane = iota((8, 128), 1)
    counts = jnp.zeros((8, 128), F32)
    dense = jnp.zeros((8, 128), F32)
    for i in range(8):
        counts = counts + jnp.where(lane == i, jnp.sum(m_in[i].astype(F32), axis=1, keepdims=True), 0.0)
        rho[i] = 0.8 * s_in[i] - 0.2 * t_in[i]
        column = jnp.sum(rho[i], axis=1, keepdims=True)
        dense = dense + jnp.where(lane == i + 8, column, 0.0)
    d_own[...] = dense
    above = rdma(d_own, d_peer, ss.at[5], sr.at[5], peer)
    above.start()
    fill(b_own, (rho,), 384)
    fill(t_own, (t_in, s_in), 512)

    loads[5].wait()

    def spread(t, carry):
        for i in range(8):
            se[t, 4 + i, 8:72, :] = sp_in[t, pl.ds(i, 64, stride=8), :]
        return carry

    lax.fori_loop(0, 4, spread, 0)
    near = pl.multiple_of((1 - lev) * 56 + 8, 8)
    there = pl.multiple_of(lev * 72, 8)
    own_x = rdma(se.at[:, 8:12, 8:72], se.at[:, 0:4, 8:72], ss.at[0], sr.at[0], xup)
    own_y = rdma(se.at[:, 4:8, 8:72], se.at[:, 12:16, 8:72], ss.at[1], sr.at[1], xdn)
    parts = [
        rdma(se.at[:, low:high, pl.ds(near, 8)], se.at[:, low:high, pl.ds(there, 8)], ss.at[i], sr.at[i], peer)
        for i, low, high in ((2, 4, 12), (3, 0, 4), (4, 12, 16))
    ]
    above.wait_recv()
    b_own[:, 256:384] = counts + jnp.where(lev == 1, d_peer[...], 0.0)
    begin(1, b_own)
    near_water = [
        rdma(t_own, gt.at[z], ts.at[0], tr.at[0], zup),
        rdma(t_own, gt.at[z], ts.at[1], tr.at[1], zdn),
        rdma(t_own.at[:, 512:], lt.at[z], ts.at[2], tr.at[2], xup),
        rdma(t_own.at[:, :512], ht.at[z], ts.at[3], tr.at[3], xdn),
    ]
    for copy in near_water:
        copy.start()
    gt[z] = t_own[...]
    own_x.start()
    own_y.start()
    parts[0].start()

    def clear(t, carry):
        se[t, :, pl.ds(there, 8), :] = jnp.zeros((16, 8, 128), F32)
        return carry

    lax.fori_loop(0, 4, clear, 0)
    half = nz // 2
    for step in range(1, half + 1):
        came = []
        for k in range(2):
            for way, source in ((0, (z + nz - step) % nz), (1, (z + step) % nz))[: 2 if step < half else 1]:
                block = wholes[k].at[source]
                along(k, block, source, way, 1).wait_recv()
                if step % 2 == 0:
                    for hop in (2, 1):
                        if step + hop <= half - way:
                            along(k, block, source, way, hop).start()
                came.append((k, block, source))
        for k, block, source in came:
            to_right(k, block, source).start()
            to_left(k, block, source).start()
        if step == 3:
            own_x.wait_recv()
            parts[1].start()
            own_y.wait_recv()
            parts[2].start()

    for part in parts:
        part.wait_recv()
        part.wait_send()

    for k in range(2):
        for ref, send, recv in ((lefts[k], ls, lr), (rights[k], hs, hr)):
            copies = rdma(ref, ref, send.at[k], recv.at[k], xup)
            copies.wait_recv()
            copies.wait_send()
        blocks = wholes[k].at[0 : nz - 1]
        rdma(blocks, blocks, zs.at[k], zr.at[k, z], zup).wait_send()
    for copy in near_water:
        copy.wait_recv()
        copy.wait_send()
    for copy in (own_x, own_y, above):
        copy.wait_send()


def flow_kernel(ga, gb, gt, la, lb, lt, ha, hb, ht, uf_ref, vf_ref, fv_ref, t_ref, s_ref, bnd_ref, uu, vv, rho, pp, cnt, top):
    lev = lax.axis_index("lev")
    sides = (
        ((uu, vv), ((la, 0), (ga, 0), (ga, 512), (ha, 0))),
        ((t_ref, s_ref), ((lt, 0), (gt, 0), (gt, 512), (ht, 0))),
        ((rho,), ((lb, 128), (gb, 0), (gb, 384), (hb, 0))),
    )
    for fields, sources in sides:
        for part, (ref, base) in enumerate(sources):
            for f, out in enumerate(fields):
                for k in range(2):
                    off = base + f * 256 + k * 128
                    r = part * 4 + k * 2
                    out[r : r + 2] = ref[:, :, off : off + 128].reshape(128, 128).T.reshape(2, 64, 128)
    aux = gb[:, :, 256:384].reshape(128, 128).T
    aux_l = lb[:, :, 0:128].reshape(128, 128).T
    aux_h = hb[:, :, 256:384].reshape(128, 128).T
    cnt[0:4], cnt[4:12], cnt[12:16] = aux_l[4:8], aux[0:8], aux_h[0:4]
    top[0:4], top[4:12], top[12:16] = aux_l[12:16], aux[8:16], aux_h[8:12]

    row, col = iota((64, 64), 0), iota((64, 64), 1)
    down = jnp.where(col < row, 1.0, jnp.where(col == row, 0.5, 0.0)).astype(BF16)
    down = jnp.concatenate([down] * 3, axis=1)
    deep = jnp.where(col >= row, 1.0, 0.0).astype(BF16)
    deep = jnp.concatenate([deep] * 3, axis=1)
    for r in range(16):
        total = jnp.dot(down, jnp.concatenate(pieces(rho[r]), axis=0), preferred_element_type=F32)
        pp[r] = buoyancy * (top[r : r + 1] + total)

    level = iota((64, 128), 0).astype(F32)
    uf_ref[0] = jnp.zeros((64, 128), F32)
    vf_ref[0] = jnp.zeros((64, 128), F32)
    for r in (14, 15):
        uf_ref[r] = jnp.zeros((64, 128), F32)
        vf_ref[r] = jnp.zeros((64, 128), F32)
    for r in range(1, 14):
        here, east = cnt[r : r + 1], cnt[r + 1 : r + 2]
        north = pltpu.roll(jnp.broadcast_to(here, (8, 128)), 127, 1)[0:1]
        p, u, v = pp[r], uu[r], vv[r]
        lap_u = uu[r + 1] + uu[r - 1] + pltpu.roll(u, 127, 1) + pltpu.roll(u, 1, 1) - 4.0 * u
        lap_v = vv[r + 1] + vv[r - 1] + pltpu.roll(v, 127, 1) + pltpu.roll(v, 1, 1) - 4.0 * v
        new_u = u + marine_advance * (p - pp[r + 1] + viscosity * lap_u)
        new_v = v + marine_advance * (p - pltpu.roll(p, 127, 1) + viscosity * lap_v)
        uf_ref[r] = jnp.where(level < jnp.minimum(here, east), new_u, 0.0)
        vf_ref[r] = jnp.where(level < jnp.minimum(here, north), new_v, 0.0)

    zero = jnp.zeros((1, 128), F32)
    first = lev == 0
    for r in range(16):
        if 2 <= r < 14:
            u, v = uf_ref[r], vf_ref[r]
            div = u - uf_ref[r - 1] + v - pltpu.roll(v, 1, 1)
            fv = jnp.dot(deep, jnp.concatenate(pieces(div), axis=0), preferred_element_type=F32)
            fv_ref[r] = fv
            flow = fv[0:1]
        else:
            fv_ref[r] = jnp.zeros((64, 128), F32)
            flow = zero
        u2 = jnp.where(first, uf_ref[r, 62:64], uf_ref[r, 0:2])
        v2 = jnp.where(first, vf_ref[r, 62:64], vf_ref[r, 0:2])
        t1 = jnp.where(first, t_ref[r, 63:64], t_ref[r, 0:1])
        s1 = jnp.where(first, s_ref[r, 63:64], s_ref[r, 0:1])
        bnd_ref[r] = jnp.concatenate([u2, v2, flow, t1, s1, zero], axis=0)


def fill_matrix(c_ref, guild_ref, light_ref, w_ref):
    kinds = iota((8, 64), 0) == guild_ref[...]
    light = jnp.sum(jnp.where(iota((8, 8), 0) == iota((8, 8), 1), light_ref[...], 0.0), axis=1, keepdims=True)
    absorb = jnp.sum(jnp.where(kinds, light, 0.0), axis=0, keepdims=True)
    absorb = jnp.broadcast_to(absorb, (8, 64))
    place, across = iota((512, 64), 0), iota((64, 512), 1)
    spread = jnp.where(place // 8 % 16 * 4 + place // 128 == iota((512, 64), 1), 1.0, 0.0).astype(BF16)
    across = jnp.where(across // 8 % 16 * 4 + across // 128 == iota((64, 512), 0), 1.0, 0.0).astype(BF16)
    tall = jnp.dot(spread, c_ref[...], preferred_element_type=F32).astype(BF16)
    wide = jnp.dot(tall, across, preferred_element_type=F32)
    w_ref[0:512] = jnp.where(iota((512, 512), 0) % 8 == iota((512, 512), 1) % 8, wide, 0.0).astype(BF16)
    own = iota((8, 512), 0) == iota((8, 512), 1) % 8
    rows = []
    for part in pieces(absorb):
        line = jnp.dot(part, across, preferred_element_type=F32)
        rows.append(jnp.where(own, line, 0.0))
    rows.append(jnp.zeros((8, 512), F32))
    w_ref[512:544] = jnp.concatenate(rows, axis=0).astype(BF16)


def react_kernel(
    nz, uf_ref, vf_ref, fv_ref, t_ref, s_ref, edge_ref, se_ref, c_ref, guild_ref, light_ref,
    adv_ref, back_ref, scale_ref, att_ref, attp_ref, oc_ref, adv_out, att_out, oc_out, out_sems,
    up, um, vp, vm, fp, fm, q1, ex, tr, yd, vpt, vmt, vpu, vmu, rest, bnd_ref, w_ref, send_ref, got, res, sizes,
    s1, r1, s2, r2, s3, r3, s4, r4, s5, r5,
):
    z, lev = lax.axis_index("trc"), lax.axis_index("lev")
    first = lev == 0
    sub = iota((8, 128), 0)
    peer = {"lev": 1 - lev}
    def rdma(src, dst, send, recv, to):
        return pltpu.make_async_remote_copy(
            src_ref=src, dst_ref=dst, send_sem=send, recv_sem=recv, device_id=to, device_id_type=MESH
        )

    def each(body):
        def one(i, carry):
            d = nz // 2 + (i + 1) // 2 * (1 - i % 2 * 2)
            body((z + d) % nz)
            return carry

        lax.fori_loop(0, nz - 1, one, 0)

    others = pl.ds(0, nz - 1)

    def to_device(to):
        return peer if to is others else {"trc": to}

    def out(t, to, at):
        return rdma(send_ref.at[t, to], got.at[t, at], s1.at[t], r1.at[t], to_device(to))

    def last(c, to, at):
        lanes = slice(c * 128, c * 128 + 128)
        return rdma(send_ref.at[2:4, to, :, lanes], got.at[2:4, at, :, lanes], s5.at[c], r5.at[c], to_device(to))

    def home(c, to, at):
        return rdma(res.at[c, :, to], back_ref.at[c, :, at], s2.at[c], r2.at[c], to_device(to))

    def size(c, to, at):
        return rdma(sizes.at[c, to], scale_ref.at[c, at], s4.at[c], r4.at[c], to_device(to))


    def stored(t):
        return pltpu.make_async_copy(adv_ref.at[t], adv_out.at[t], out_sems.at[t])

    def own_back(c):
        return pltpu.make_async_copy(res.at[c, :, z], back_ref.at[c, :, z], out_sems.at[4 + c])

    def own_scale(c):
        return pltpu.make_async_copy(sizes.at[c, z], scale_ref.at[c, z], out_sems.at[8 + c])

    ocean = pltpu.make_async_copy(oc_ref, oc_out, out_sems.at[12])
    shades = pltpu.make_async_copy(att_ref, att_out, out_sems.at[13])
    edges = rdma(edge_ref.at[1:14], bnd_ref.at[1:14], s3.at[0], r3.at[0], peer)
    edges.start()
    mine = pl.multiple_of(z * 8, 8)
    for f, ref in enumerate((uf_ref, vf_ref)):
        for k in range(4):
            tr[...] = ref[4 + 2 * k : 6 + 2 * k].reshape(128, 128).T
            oc_ref[2 + f, :, k * 128 : k * 128 + 128] = tr[pl.ds(mine, 8), :]
    fill_matrix(c_ref, guild_ref, light_ref, w_ref)
    bnd_ref[0] = jnp.zeros((8, 128), F32)
    edges.wait_recv()

    def rows(r):
        return pl.ds(pl.multiple_of(r * 80, 8), 80)

    def around(own, above, below):
        return jnp.concatenate(
            [jnp.where(first, 0.0, above), own, jnp.where(first, below, 0.0)], axis=0
        )

    def faces(r, carry):
        edge = bnd_ref[r]
        edge_w = bnd_ref[r - 1]
        pos = pltpu.roll(edge, 6, 0)
        u_ext = around(uf_ref[r], jnp.where(sub >= 6, pos, 0.0), jnp.where(sub < 2, edge, 0.0))
        two = pltpu.roll(edge, 4, 0)
        low = pltpu.roll(edge, 6, 0)
        v_ext = around(vf_ref[r], jnp.where(sub >= 6, two, 0.0), jnp.where(sub < 2, low, 0.0))
        d2 = edge[0:2] - edge_w[0:2] + edge[2:4] - pltpu.roll(edge, 1, 1)[2:4]
        d0, d1 = d2[0:1], d2[1:2]
        flow = jnp.where(first, edge[4:5], 0.0)
        f_own = fv_ref[r] + flow
        above = jnp.where(sub == 7, f_own[0:1] + d1, jnp.where(sub == 6, f_own[0:1] + d1 + d0, 0.0))
        below = jnp.where(
            sub == 0, flow, jnp.where(sub == 1, flow - d0, jnp.where(sub == 2, flow - d0 - d1, 0.0))
        )
        surface = jnp.where((iota((64, 128), 0) == 0) & first, 0.0, f_own)
        f_ext = level_step * around(surface, above, below)
        u_ext = tracer_step * u_ext
        v_ext = tracer_step * v_ext
        up[r], um[r] = jnp.maximum(u_ext, 0.0), jnp.minimum(u_ext, 0.0)
        vp[rows(r)], vm[rows(r)] = jnp.maximum(v_ext, 0.0), jnp.minimum(v_ext, 0.0)
        fp[r], fm[r] = jnp.maximum(f_ext, 0.0), jnp.minimum(f_ext, 0.0)
        return carry

    lax.fori_loop(1, 14, faces, 0)

    def turn_faces(ref, wide, narrow):
        for c in range(9):
            wide[c] = ref[64 + 128 * c : 192 + 128 * c].T
        for k in range(4):
            row = (4 + 2 * k) * 80 + 8
            both = jnp.concatenate([ref[row : row + 64], ref[row + 80 : row + 144]], axis=0)
            narrow[k] = both.T

    turn_faces(vp, vpt, vpu)
    turn_faces(vm, vmt, vmu)

    def along_y(q, plus, minus):
        north = 0.5 * (pltpu.roll(q, 127, 0) - q)
        slope = minmod_half(pltpu.roll(north, 1, 0), north)
        flux = plus * (q + slope) + minus * pltpu.roll(q - slope, 127, 0)
        return flux - pltpu.roll(flux, 1, 0)

    def sweep(load, store, start, stop):
        d_a = 0.5 * (load(start - 1) - load(start - 2))
        d_b = 0.5 * (load(start) - load(start - 1))
        d_c = 0.5 * (load(start + 1) - load(start))
        right = load(start - 1) + minmod_half(d_a, d_b)
        slope = minmod_half(d_b, d_c)
        flux = up[start - 1] * right + um[start - 1] * (load(start) - slope)

        def one(r, carry):
            d_here, right, flux = carry
            q, q_e = load(r), load(r + 1)
            d_next = 0.5 * (load(r + 2) - q_e)
            slope = minmod_half(d_here, d_next)
            flux_e = up[r] * right + um[r] * (q_e - slope)
            change = flux_e - flux
            right_e = q_e + slope
            below = 0.5 * (pltpu.roll(q, 79, 0) - q)
            slope = minmod_half(pltpu.roll(below, 1, 0), below)
            flux_v = fp[r] * pltpu.roll(q + slope, 1, 0) + fm[r] * (q - slope)
            change = change + (pltpu.roll(flux_v, 79, 0) - flux_v)
            store(r, q - change)
            return d_next, right_e, flux_e

        lax.fori_loop(start, stop, one, (d_c, load(start) + slope, flux))

    def tracer(t, carry):
        def first_load(r):
            return se_ref[t, r]

        def first_store(r, value):
            q1[rows(r)] = value - yd[rows(r)]

        def second_load(r):
            return q1[rows(r)]

        def second_store(r, value):
            rest[r - 4] = value[8:72]

        for c in range(9):
            start, stop = 64 + 128 * c, 192 + 128 * c
            q = [se_ref[t, r, max(start - r * 80, 0) : min(stop - r * 80, 80)] for r in range(start // 80, (stop + 79) // 80)]
            q = jnp.concatenate(q, axis=0).T
            yd[64 + 128 * c : 192 + 128 * c] = along_y(q, vpt[c], vmt[c]).T
        sweep(first_load, first_store, 2, 14)
        sweep(second_load, second_store, 4, 12)
        for k in range(4):
            row = (4 + 2 * k) * 80 + 8
            q = jnp.concatenate([q1[row : row + 64], q1[row + 80 : row + 144]], axis=0).T
            new = rest[2 * k : 2 * k + 2].reshape(128, 128).T - along_y(q, vpu[k], vmu[k])
            adv_ref[t, k] = new
            send_ref[t, :, :, k * 128 : k * 128 + 128] = new.reshape(16, 8, 128).astype(BF16)

        @pl.when(t < 2)
        def _():
            each(lambda to: out(t, to, z).start())

        got[t, z] = send_ref[t, z]
        stored(t).start()
        return carry

    lax.fori_loop(0, 4, tracer, 0)
    for c in range(4):
        each(lambda to: last(c, to, z).start())

    for f, ref in enumerate((t_ref, s_ref)):
        for r in range(3, 13):
            edge = bnd_ref[r][5 + f : 6 + f]
            ex[r] = around(ref[r], jnp.where(sub == 7, edge, 0.0), jnp.where(sub == 0, edge, 0.0))

        def donor(r, flux_w):
            c = ex[r]
            flux = up[r] * c + um[r] * ex[r + 1]
            flux_n = vp[rows(r)] * c + vm[rows(r)] * pltpu.roll(c, 127, 1)
            flux_v = fp[r] * pltpu.roll(c, 1, 0) + fm[r] * c
            wide = flux - flux_w + (flux_n - pltpu.roll(flux_n, 1, 1))
            tall = pltpu.roll(flux_v, 79, 0) - flux_v
            new = c - (marine_advance / tracer_step) * wide - (marine_advance / level_step) * tall
            q1[rows(r)] = new
            return flux

        lax.fori_loop(4, 12, donor, up[3] * ex[3] + um[3] * ex[4])
        for k in range(4):
            row = (4 + 2 * k) * 80 + 8
            both = jnp.concatenate([q1[row : row + 64], q1[row + 80 : row + 144]], axis=0)
            tr[...] = both.T
            oc_ref[f, :, k * 128 : k * 128 + 128] = tr[pl.ds(mine, 8), :]
    ocean.start()

    for t in range(2):
        out(t, others, others).wait_recv()
    for c in range(4):
        last(c, others, others).wait_recv()
        values = got[:, :, :, c * 128 : c * 128 + 128].reshape(512, 128)
        values = jnp.dot(w_ref[...], values, preferred_element_type=F32)
        att_ref[c] = values[512:520] + values[520:528] + values[528:536]
        values = values[0:512].reshape(4, nz, 8, 128)
        largest = jnp.max(jnp.max(jnp.abs(values), axis=0), axis=1, keepdims=True)
        largest = jnp.maximum(largest, 1e-30)
        sizes[c] = largest * (1.0 / 32767.0)
        coded = jnp.round(values * (32767.0 / largest)[None])
        res[c] = coded.astype(jnp.int32).astype(I16)
        each(lambda to: (home(c, to, z).start(), size(c, to, z).start()))
        own_back(c).start()
        own_scale(c).start()
    shade = rdma(att_ref, attp_ref, s3.at[1], r3.at[1], peer)
    shade.start()
    shades.start()
    for c in range(4):
        home(c, others, others).wait_recv()
        size(c, others, others).wait_recv()
        last(c, others, others).wait_send()
        if c < 2:
            out(c, others, others).wait_send()
        home(c, others, others).wait_send()
        size(c, others, others).wait_send()
    shade.wait_recv()
    shade.wait_send()
    edges.wait_send()
    for c in range(4):
        stored(c).wait()
        own_back(c).wait()
        own_scale(c).wait()
    ocean.wait()
    shades.wait()


GATHERED = 10
LOADED = 11
ARRIVALS = 11
FLOWS = 6


def step_kernel(nz, nx, *refs):
    fields, params, outs, scratch = refs[:6], refs[6:9], refs[9:15], refs[15:]
    gathered, scratch = scratch[:GATHERED], scratch[GATHERED:]
    loaded, scratch = scratch[: LOADED + ARRIVALS], scratch[LOADED + ARRIVALS :]
    flows, scratch = scratch[:FLOWS], scratch[FLOWS:]
    temporary, scratch = scratch[:6], scratch[6:]
    held, scratch = scratch[:3], scratch[3:]
    param_sems, out_sems, adv_ref, att_ref, oc_ref = scratch[:5]
    loads = [pltpu.make_async_copy(src, dst, param_sems.at[i]) for i, (src, dst) in enumerate(zip(params, held))]
    for load in loads:
        load.start()
    gather_kernel(nz, nx, *fields, *gathered, *loaded)
    flow_kernel(*gathered[:9], *flows, *temporary)
    for load in loads:
        load.wait()
    adv_out, back_ref, scale_ref, att_out, attp_ref, oc_out = outs
    react_kernel(
        nz, *flows, gathered[9], *held, adv_ref, back_ref, scale_ref, att_ref, attp_ref, oc_ref,
        adv_out, att_out, oc_out, out_sems, *scratch[5:]
    )


def final_kernel(
    adv_hbm, back_hbm, scale_hbm, att_hbm, attp_hbm, oc_hbm, m_hbm,
    w_hbm, s_hbm, u_hbm, v_hbm, sp_hbm,
    adv_ref, back_ref, scale_ref, att_ref, attp_ref, oc_ref, m_ref, w_ref, s_ref, u_ref, v_ref, sp_ref,
    ins, outs,
):
    lev = lax.axis_index("lev")
    smalls = [
        pltpu.make_async_copy(src, dst, ins.at[i])
        for i, (src, dst) in enumerate(
            ((scale_hbm, scale_ref), (att_hbm, att_ref), (attp_hbm, attp_ref), (oc_hbm, oc_ref), (m_hbm, m_ref))
        )
    ]
    backs = [pltpu.make_async_copy(back_hbm.at[:, t], back_ref.at[:, t], ins.at[5 + t]) for t in range(4)]
    advs = [pltpu.make_async_copy(adv_hbm.at[t], adv_ref.at[t], ins.at[9 + t]) for t in range(4)]
    for copy in smalls:
        copy.start()
    for t in range(4):
        backs[t].start()
        advs[t].start()
    for copy in smalls:
        copy.wait()
    row, col = iota((128, 128), 0), iota((128, 128), 1)
    same = row // 64 == col // 64
    before = jnp.where(same & (row < col), 1.0, 0.0).astype(BF16)
    every = jnp.where(same & (lev == 1), 1.0, 0.0).astype(BF16)
    sums = jnp.concatenate([before] * 3 + [every] * 3, axis=0)
    for c in range(4):
        att = att_ref[c]
        terms = jnp.concatenate(pieces(att) + pieces(attp_ref[c]), axis=1)
        path = jnp.dot(terms, sums, preferred_element_type=F32)
        caught = jnp.exp(-path) * (1.0 - jnp.exp(-att))
        wet = jnp.concatenate([m_ref[2 * c], m_ref[2 * c + 1]], axis=1).astype(F32)
        lanes = slice(c * 128, c * 128 + 128)
        warm = oc_ref[0, :, lanes] + warming_amount * wet * caught
        for out, value in ((w_ref, warm), (s_ref, oc_ref[1, :, lanes]), (u_ref, oc_ref[2, :, lanes]), (v_ref, oc_ref[3, :, lanes])):
            out[2 * c] = value[:, 0:64]
            out[2 * c + 1] = value[:, 64:128]
    done = [
        pltpu.make_async_copy(src, dst, outs.at[i])
        for i, (src, dst) in enumerate(((w_ref, w_hbm), (s_ref, s_hbm), (u_ref, u_hbm), (v_ref, v_hbm)))
    ]
    for copy in done:
        copy.start()
    for t in range(4):
        backs[t].wait()
        advs[t].wait()
        for c in range(4):
            react = back_ref[c, t].astype(jnp.int32).astype(F32) * scale_ref[c]
            new = (adv_ref[t, c] + react_step * react.reshape(128, 128)).T
            sp_ref[t, pl.ds(2 * c, 64, stride=8), :] = new[0:64]
            sp_ref[t, pl.ds(2 * c + 1, 64, stride=8), :] = new[64:128]
        done.append(pltpu.make_async_copy(sp_ref.at[t], sp_hbm.at[t], outs.at[4 + t]))
        done[-1].start()
    for copy in done:
        copy.wait()


def shards(
    nz,
    nx,
    potential_warmth,
    saltiness_anomaly,
    zonal_speed,
    meridional_speed,
    marine_indicator,
    species_concentrations,
    coupling_matrix,
    species_guild_number,
    guild_extinction_coefficient,
):
    tiles = [
        jnp.transpose(a, (1, 2, 0))
        for a in (potential_warmth, saltiness_anomaly, zonal_speed, meridional_speed, marine_indicator)
    ]
    species = species_concentrations.reshape(4, 512, 128)
    dma = pltpu.SemaphoreType.DMA
    tile = pltpu.VMEM((8, 8, 64), F32)
    row, column = pltpu.VMEM((16, 64, 128), F32), pltpu.VMEM((16, 128), F32)
    tall, flat = pltpu.VMEM((16, 80, 128), F32), pltpu.VMEM((1280, 128), F32)
    edge = pltpu.VMEM((16, 8, 128), F32)
    adv, back, scale, att, attp, ocean = pl.pallas_call(
        functools.partial(step_kernel, nz, nx),
        out_shape=(
            sds((4, 4, 128, 128)),
            sds((4, 4, nz, 8, 128), I16),
            sds((4, nz, 1, 128)),
            sds((4, 8, 128)),
            sds((4, 8, 128)),
            sds((4, 8, 512)),
        ),
        in_specs=[pl.BlockSpec(memory_space=pltpu.HBM)] * 9,
        out_specs=(pl.BlockSpec(memory_space=pltpu.HBM),) * 6,
        scratch_shapes=[pltpu.VMEM((nz, 8, lanes), F32) for lanes in (SPEEDS, DENSITY, WATER, 512, 384, 512, 512, 384, 512)]
        + [pltpu.VMEM((4, 16, 80, 128), F32)]
        + [tile] * 4
        + [
            pltpu.VMEM((8, 8, 64), jnp.int32),
            pltpu.VMEM((4, 512, 128), F32),
            pltpu.VMEM((8, SPEEDS), F32),
            pltpu.VMEM((8, DENSITY), F32),
            pltpu.VMEM((8, WATER), F32),
            pltpu.VMEM((8, 128), F32),
            pltpu.VMEM((8, 128), F32),
            dma((6,)),
            dma((2,)),
            dma((2, nz)),
        ]
        + [dma((2,))] * 4
        + [dma((6,))] * 2
        + [dma((4,))] * 2
        + [row] * 5
        + [edge, row, row, row, row, column, column]
        + [
            pltpu.VMEM((64, 64), BF16),
            pltpu.VMEM((1, 64), jnp.int32),
            pltpu.VMEM((1, 8), F32),
            dma((3,)),
            dma((14,)),
            pltpu.VMEM((4, 4, 128, 128), F32),
            pltpu.VMEM((4, 8, 128), F32),
            pltpu.VMEM((4, 8, 512), F32),
        ]
        + [tall, tall, flat, flat, tall, tall, flat, tall]
        + [
            pltpu.VMEM((128, 128), F32),
            flat,
            pltpu.VMEM((9, 128, 128), F32),
            pltpu.VMEM((9, 128, 128), F32),
            pltpu.VMEM((4, 128, 128), F32),
            pltpu.VMEM((4, 128, 128), F32),
            pltpu.VMEM((8, 64, 128), F32),
            edge,
            pltpu.VMEM((544, 512), BF16),
            pltpu.VMEM((4, nz, 8, 512), BF16),
            pltpu.VMEM((4, nz, 8, 512), BF16),
            pltpu.VMEM((4, 4, nz, 8, 128), I16),
            pltpu.VMEM((4, nz, 1, 128), F32),
        ]
        + [dma((4,))] * 4
        + [dma((2,))] * 2
        + [dma((4,))] * 4,
        compiler_params=pltpu.CompilerParams(collective_id=0, has_side_effects=True, vmem_limit_bytes=60 << 20),
        name="step",
    )(
        *tiles, species, coupling_matrix,
        species_guild_number.reshape(1, 64), guild_extinction_coefficient.reshape(1, 8),
    )

    hbm = pl.BlockSpec(memory_space=pltpu.HBM)
    warm, salt, zonal, merid, final = pl.pallas_call(
        final_kernel,
        out_shape=(sds((8, 8, 64)),) * 4 + (sds((4, 512, 128)),),
        in_specs=[hbm] * 7,
        out_specs=(hbm,) * 5,
        scratch_shapes=[
            pltpu.VMEM((4, 4, 128, 128), F32),
            pltpu.VMEM((4, 4, nz, 8, 128), I16),
            pltpu.VMEM((4, nz, 1, 128), F32),
            pltpu.VMEM((4, 8, 128), F32),
            pltpu.VMEM((4, 8, 128), F32),
            pltpu.VMEM((4, 8, 512), F32),
            pltpu.VMEM((8, 8, 64), jnp.int32),
        ]
        + [tile] * 4
        + [pltpu.VMEM((4, 512, 128), F32), dma((13,)), dma((8,))],
        compiler_params=pltpu.CompilerParams(vmem_limit_bytes=60 << 20),
        name="final",
    )(adv, back, scale, att, attp, ocean, tiles[4])
    warm, salt, zonal, merid = (jnp.transpose(a, (2, 0, 1)) for a in (warm, salt, zonal, merid))
    return warm, salt, zonal, merid, final.reshape(4, 64, 8, 128)


def solution(mesh):
    tile, tracers = P("lev", "cols", "trc"), P("trc", "lev", "cols", None)
    return jax.shard_map(
        functools.partial(shards, mesh.shape["trc"], mesh.shape["cols"]),
        mesh=mesh,
        in_specs=(tile, tile, tile, tile, tile, tracers, P(), P(), P()),
        out_specs=(tile, tile, tile, tile, tracers),
        check_vma=False,
    )
```
